32 devices in a mesh: rows: 16 (over z, y, x), cols: 2 (over core).
Axes of the slice: x: 2, y: 2, z: 4, core: 2. Of those that a mesh axis runs over, the one named last changes fastest.
Arguments:
- parent_front: float32 [4096, 2048], P('rows', 'cols')
- right_sides: float32 [4096, 64], P('rows'), may hold values from -6 to 6
- child_values: float32 [1024, 1024], P('rows', 'cols'), may hold values from -6 to 6
- block_owner: int32 [256], P('rows'), may hold values from 0 to 15, as said below
- row_map: int32 [1024], P('rows'), may hold values from 0 to 255
- col_map: int32 [1024], P('cols'), may hold values from 0 to 1023, as said below
Outputs:
- updated: float32 [4096, 2048], P('rows', 'cols')
- side_coeffs: float32 [128, 64], replicated
- side_left: float32 [4096, 64], P('rows')
The draws below stay inside these ranges and needn't reach their ends.
Inputs may be any that keep to these rules, and one draw needn't show every extreme that they name: `block_owner`: for every k, entries k * 16 to (k + 1) * 16 - 1 form a permutation of 0 to 15. `col_map`: each aligned run of 512 entries is strictly increasing, starts with 0 and ends with 1023.
All inputs are finite; a program needn't handle non-finite values.
Results may differ from the reference program's by a relative error of at most 0.0003.
Values sent between devices are 32-bit elements; how exact they have to be, the bound alone decides.
A program may use at most 64 MiB of HBM per device.

```python
import math
import jax
import jax.numpy as jnp
from jax import lax

R_DEV = 256
C_DEV = 1024
PANEL = 128
RHS = 64
RBLOCKS = 16
NR = 4096
NC = 2048
BLK = 4
CH_ROWS = 1024
CC_DEV = 512
CHC = 1024


def draw_parent_front(key, part):
    keys = jax.random.split(key, 3)
    entries = jax.random.normal(keys[0], (NR, NC), jnp.float32)
    trailing = (jnp.arange(NC) >= PANEL).astype(jnp.float32)[None, :]
    rising = jnp.exp(math.log(3.0) * jnp.arange(NR, dtype=jnp.float32) / NR)[:, None]
    row_scale = 0.4 * jnp.exp(math.log(10.0) * jax.random.uniform(keys[1], (NR, 1), jnp.float32)) * rising
    col_spread = 0.3 * jnp.exp(math.log(10.0) * jax.random.uniform(keys[2], (1, NC), jnp.float32))
    col_scale = trailing * col_spread + (1.0 - trailing)
    return entries * row_scale * col_scale


def draw_block_owner(key, part):
    keys = jax.random.split(jax.random.fold_in(key, 11), RBLOCKS)
    table = jax.vmap(lambda single: jax.random.permutation(single, RBLOCKS))(keys)
    return table.reshape(-1).astype(jnp.int32)


def single_map(key):
    chosen = jax.random.permutation(key, C_DEV - 2)[:CC_DEV - 2] + 1
    inner = jnp.sort(chosen).astype(jnp.int32)
    first = jnp.zeros((1,), jnp.int32)
    final = jnp.full((1,), C_DEV - 1, jnp.int32)
    return jnp.concatenate([first, inner, final])


def draw_col_map(key, part):
    keys = jax.random.split(jax.random.fold_in(key, 23), CHC // CC_DEV)
    return jax.vmap(single_map)(keys).reshape(-1).astype(jnp.int32)


def with_ends(values, stream_key, least, largest):
    dims = values.shape
    spot = [jax.random.randint(jax.random.fold_in(stream_key, axis), (), 0, dims[axis]) for axis in range(len(dims))]
    values = values.at[tuple(spot)].set(least)
    longest = dims.index(max(dims))
    spot[longest] = (spot[longest] + 1) % dims[longest]
    return values.at[tuple(spot)].set(largest)


def block_scale(own_key, shape, cuts, smallest, largest):
    factor_of, own = 1.0, jax.random.fold_in(own_key, 6)
    for axis_at, blocks in cuts:
        heights = jnp.exp(jax.random.uniform(jax.random.fold_in(own, axis_at), (blocks,), jnp.float32, smallest / len(cuts), largest / len(cuts)))
        factor_of = factor_of * jnp.repeat(heights, shape[axis_at] // blocks).reshape([-1 if axis == axis_at else 1 for axis in range(len(shape))])
    return factor_of


def bell_draw(stream_key, shape, width, bound, shards=(), kind=jnp.bfloat16):
    result = width * jax.random.normal(stream_key, shape, jnp.float32)
    if shards:
        result = result * block_scale(stream_key, shape, shards, -0.22, 0.18)
    return jnp.clip(result, -bound, bound).astype(kind)


def setup_inputs(seed: int = 0) -> dict:
    key_list = jax.random.split(jax.random.key(seed), 7)
    return {
        "parent_front": draw_parent_front(jax.random.fold_in(key_list[6], 71), 0),
        "right_sides": bell_draw(key_list[1], (NR, RHS), 1.0, 6.0, ((0, 16),), jnp.float32),
        "child_values": bell_draw(key_list[2], (CH_ROWS, CHC), 1.0, 6.0, ((0, 16), (1, 2)), jnp.float32),
        "block_owner": draw_block_owner(jax.random.fold_in(key_list[6], 71), 0),
        "row_map": with_ends(jax.random.randint(key_list[4], (CH_ROWS,), 0, R_DEV), jax.random.fold_in(key_list[4], 1), 0, R_DEV - 1).astype(jnp.int32),
        "col_map": draw_col_map(jax.random.fold_in(key_list[6], 71), 0),
    }


def reference(parent_front, right_sides, child_values, block_owner, row_map, col_map):
    child_index = jnp.arange(CH_ROWS, dtype=jnp.int32)
    parent_row = (block_owner[child_index // BLK] * R_DEV + row_map).astype(jnp.int32)
    column_index = jnp.arange(CHC, dtype=jnp.int32)
    parent_col = (column_index // CC_DEV * C_DEV + col_map).astype(jnp.int32)
    assembled = parent_front.at[parent_row[:, None], parent_col[None, :]].add(child_values)
    panel_rows = assembled[:, :PANEL]
    orthogonal, upper = jnp.linalg.qr(panel_rows)
    projected = jnp.dot(orthogonal.T, assembled, precision=lax.Precision.HIGHEST)
    coefs = jax.scipy.linalg.solve_triangular(upper, projected, lower=False)
    updated = assembled - jnp.dot(panel_rows, coefs, precision=lax.Precision.HIGHEST)
    side_projected = jnp.dot(orthogonal.T, right_sides, precision=lax.Precision.HIGHEST)
    side_coeffs = jax.scipy.linalg.solve_triangular(upper, side_projected, lower=False)
    side_left = right_sides - jnp.dot(panel_rows, side_coeffs, precision=lax.Precision.HIGHEST)
    return (updated, side_coeffs, side_left)
```

```python
import functools

import jax
import jax.numpy as jnp
from jax import lax
from jax.experimental import pallas as pl
from jax.experimental.pallas import tpu as pltpu
from jax.sharding import PartitionSpec as P

PANEL = 128
LANES = 128
SUBLANES = 8
TILE = 256
VMEM_LIMIT = 33521664
MESH = pl.DeviceIdType.MESH
f32 = jnp.float32
bf16 = jnp.bfloat16


def pieces(value):
    first = value.astype(bf16)
    rest = value - first.astype(f32)
    second = rest.astype(bf16)
    third = (rest - second.astype(f32)).astype(bf16)
    return first, second, third


def dot(left, right, dims, precision=None):
    return lax.dot_general(left, right, (dims, ((), ())), precision=precision, preferred_element_type=f32)


def dot_full(left, right, dims=((1,), (0,))):
    return dot(left, right, dims, lax.Precision.HIGHEST)


def inverse_pair(a, b, d):
    ia = 1.0 / a
    ratio = b * ia
    i11 = 1.0 / (d - b * ratio)
    i01 = -ratio * i11
    return ia - ratio * i01, i01, i11


def sweep_four(mat, k, lane):
    cols = [mat[:, k + j : k + j + 1] for j in range(4)]
    rows = [mat[k + j : k + j + 1, :] for j in range(4)]
    d = [[jnp.broadcast_to(mat[k + i : k + i + 1, k + j : k + j + 1], (1, mat.shape[1])) for j in range(i + 1)] for i in range(4)]
    a00, a01, a11 = inverse_pair(d[0][0], d[1][0], d[1][1])
    l20, l21 = d[2][0] * a00 + d[2][1] * a01, d[2][0] * a01 + d[2][1] * a11
    l30, l31 = d[3][0] * a00 + d[3][1] * a01, d[3][0] * a01 + d[3][1] * a11
    s22 = d[2][2] - (l20 * d[2][0] + l21 * d[2][1])
    s32 = d[3][2] - (l30 * d[2][0] + l31 * d[2][1])
    s33 = d[3][3] - (l30 * d[3][0] + l31 * d[3][1])
    e22, e32, e33 = inverse_pair(s22, s32, s33)
    e20, e21 = -(e22 * l20 + e32 * l30), -(e22 * l21 + e32 * l31)
    e30, e31 = -(e32 * l20 + e33 * l30), -(e32 * l21 + e33 * l31)
    e00 = a00 - (l20 * e20 + l30 * e30)
    e10 = a01 - (l21 * e20 + l31 * e30)
    e11 = a11 - (l21 * e21 + l31 * e31)
    e = [[e00, e10, e20, e30], [e10, e11, e21, e31], [e20, e21, e22, e32], [e30, e31, e32, e33]]
    lane_row = lane[:1]
    tops = []
    for i in range(4):
        top = (e[i][0] * rows[0] + e[i][1] * rows[1]) + (e[i][2] * rows[2] + e[i][3] * rows[3])
        for j in range(4):
            top = jnp.where(lane_row == k + j, -e[i][j], top)
        tops.append(top)
    out = jnp.where((lane >= k) & (lane < k + 4), 0.0, mat)
    out = out - ((cols[0] * tops[0] + cols[1] * tops[1]) + (cols[2] * tops[2] + cols[3] * tops[3]))
    head = out[:SUBLANES]
    sub = lax.broadcasted_iota(jnp.int32, head.shape, 0)
    for j in range(4):
        head = jnp.where(sub == k + j, tops[j], head)
    return jnp.concatenate([head, out[SUBLANES:]], axis=0)


def sweep_groups(mat, count):
    size = mat.shape[0]
    lane = lax.broadcasted_iota(jnp.int32, mat.shape, 1)

    def group(_, mat):
        for k in range(0, SUBLANES, 4):
            mat = sweep_four(mat, k, lane)
        mat = jnp.concatenate([mat[SUBLANES:], mat[:SUBLANES]], axis=0)
        return pltpu.roll(mat, size - SUBLANES, 1)

    return lax.fori_loop(0, count, group, mat)


def plan(n, width):
    levels = n.bit_length() - 1
    halving = min(levels, (PANEL // SUBLANES).bit_length() - 1)
    nparts = min(3, levels)
    tiles = width // LANES
    starts = [tiles * q // nparts * LANES for q in range(nparts + 1)]
    orders = [[(q + t) % nparts for t in range(nparts)] + list(range(nparts, levels)) for q in range(nparts)]
    single = max(halving - 2, 0)
    cuts = [(t, t + 1) for t in range(single)] + [(single, halving)]
    parts = [([order[a:b] for a, b in cuts], [[bit] for bit in order[halving:]]) for order in orders]
    return starts, parts, halving


def slots_of(n):
    levels = n.bit_length() - 1
    halving = min(levels, (PANEL // SUBLANES).bit_length() - 1)
    rows, count = 0, 0
    single = max(halving - 2, 0)
    size = PANEL
    for bits in [1] * single + [halving - single]:
        size >>= bits
        rows += ((1 << bits) - 1) * size
        count += (1 << bits) - 1
    rows += (levels - halving) * SUBLANES
    count += levels - halving
    return rows, count


def kernel(n, ncols, owner_hbm, parent, rhs_hbm, child_hbm, row_map_hbm, col_map_hbm,
           front, left, inverse, total, panel, owner, rhs_t, row_map, col_map, child, send, recv, flat, hot, sides, prod, halves, gram, gram_in, gram_all,
           in_sem, a2a_send, a2a_recv, pan_send, pan_recv, gram_send, gram_recv, red_send, red_recv):
    row, col = lax.axis_index("rows"), lax.axis_index("cols")
    rows_dev, cols_dev = front.shape
    child_rows, child_cols = child.shape
    nrhs = rhs_t.shape[0]
    block = child_rows // n
    first_loads = [
        pltpu.make_async_copy(source, target, in_sem.at[k])
        for k, (source, target) in enumerate([(owner_hbm, owner), (row_map_hbm, row_map), (child_hbm, child)])
    ]
    later_loads = [
        pltpu.make_async_copy(source, target, in_sem.at[3 + k])
        for k, (source, target) in enumerate([(col_map_hbm, col_map), (rhs_hbm, rhs_t), (parent, front)])
    ]
    for load in first_loads + later_loads:
        load.start()

    barrier = pltpu.get_barrier_semaphore()
    for step in range(1, n):
        pl.semaphore_signal(barrier, inc=1, device_id=(lax.rem(row + step, n), col), device_id_type=MESH)
    for step in range(1, ncols):
        pl.semaphore_signal(barrier, inc=1, device_id=(row, lax.rem(col + step, ncols)), device_id_type=MESH)

    for load in first_loads:
        load.wait()
    source = lax.broadcasted_iota(jnp.int32, (1, child_rows), 1)
    target = jnp.zeros((1, child_rows), jnp.int32)
    for k in range(n):
        target = jnp.where(source // block == k, owner[k] * block + source % block, target)
    place = lax.broadcasted_iota(jnp.int32, (child_rows, child_rows), 0) == target
    place_f = jnp.where(place, 1.0, 0.0).astype(f32)
    landing = jnp.sum(place_f * row_map[...].astype(f32), axis=1, keepdims=True)
    place_b = place_f.astype(bf16)
    one, two, three = pieces(child[...])
    ordered = dot(place_b, one, ((1,), (0,))) + dot(place_b, two, ((1,), (0,))) + dot(place_b, three, ((1,), (0,)))
    landing = jnp.broadcast_to(landing, (child_rows, LANES))
    for k in range(n):
        send[k, :, :child_cols] = ordered[k * block : (k + 1) * block]
        send[k, :, child_cols:] = landing[k * block : (k + 1) * block]

    pl.semaphore_wait(barrier, n - 1 + ncols - 1)

    copies = []
    for step in range(1, n):
        peer = lax.rem(row + step, n)
        copy = pltpu.make_async_remote_copy(
            src_ref=send.at[peer], dst_ref=recv.at[row], send_sem=a2a_send.at[step], recv_sem=a2a_recv.at[step],
            device_id=(peer, col), device_id_type=MESH)
        copy.start()
        copies.append(copy)
    recv[row] = send[row]

    for load in later_loads:
        load.wait()
    cols_at = lax.broadcasted_iota(jnp.int32, hot.shape, 0)
    hot[...] = jnp.where(cols_at == col_map[...], 1.0, 0.0).astype(f32).astype(bf16)
    padded = jnp.concatenate([rhs_t[...], jnp.zeros((sides.shape[1] - nrhs, rows_dev), f32)], axis=0)
    sides[...] = jnp.transpose(padded)
    for copy in copies:
        copy.wait()

    for k in range(n):
        flat[k * block : (k + 1) * block, :] = recv[k]
    vals = jnp.concatenate(pieces(flat[:, :child_cols]), axis=0)
    where_rows = flat[:, child_cols:].astype(jnp.int32)
    rows_at = lax.broadcasted_iota(jnp.int32, where_rows.shape, 1)
    landed = jnp.concatenate(
        [jnp.where(where_rows == rows_at + t * LANES, 1.0, 0.0).astype(f32) for t in range(rows_dev // LANES)], axis=1)
    landed3 = jnp.concatenate([landed] * 3, axis=0).astype(bf16)

    def assemble(first, last):
        spread3 = dot(vals, hot[first:last, :], ((1,), (1,)))
        spread = spread3[:child_rows] + spread3[child_rows : 2 * child_rows] + spread3[2 * child_rows :]
        stacked = jnp.concatenate(pieces(spread), axis=0)
        front[:, first:last] = front[:, first:last] + dot(landed3, stacked, ((0,), (0,)))

    assemble(0, PANEL)
    pan_copies = [
        pltpu.make_async_remote_copy(
            src_ref=front.at[:, pl.ds(0, PANEL)], dst_ref=panel, send_sem=pan_send.at[step - 1], recv_sem=pan_recv,
            device_id=(row, step), device_id_type=MESH)
        for step in range(1, ncols)
    ]

    @pl.when(col == 0)
    def _():
        for copy in pan_copies:
            copy.start()
        panel[...] = front[:, :PANEL]

    assemble(PANEL, cols_dev)

    @pl.when(col == 0)
    def _():
        for copy in pan_copies:
            copy.wait_send()

    @pl.when(col != 0)
    def _():
        pan_copies[0].wait_recv()

    block_panel = panel[...]
    trans = ((0,), (0,))
    gram[...] = dot_full(block_panel, block_panel, trans)

    chunks = min(n, PANEL // SUBLANES)
    chunk = PANEL // chunks
    own_chunk = lax.rem(row, chunks)
    own_rows = pl.ds(pl.multiple_of(own_chunk * chunk, SUBLANES), chunk)
    gathers = []
    for step in range(1, n):
        peer = lax.rem(row + step, n)
        start = pl.multiple_of(lax.rem(peer, chunks) * chunk, SUBLANES)
        copy = pltpu.make_async_remote_copy(
            src_ref=gram.at[pl.ds(start, chunk)], dst_ref=gram_in.at[row],
            send_sem=gram_send.at[step], recv_sem=gram_recv.at[step], device_id=(peer, col), device_id_type=MESH)
        copy.start()
        gathers.append(copy)
    gram_in[row] = gram[own_rows, :]

    def products(first, last):
        split = min(max(first, cols_dev), last)
        if split > first:
            prod[:, first:split] = dot_full(block_panel, front[:, first:split], trans)
        if last > split:
            prod[:, split:last] = dot_full(block_panel, sides[:, split - cols_dev : last - cols_dev], trans)

    starts, parts, halving = plan(n, prod.shape[1])
    base = [row * 0] * len(parts)
    nstages = len(parts[0][0])

    def own_bit(bit):
        return (row // (1 << bit)) % 2

    def members(bits):
        mine = sum(own_bit(bit) * (1 << i) for i, bit in enumerate(bits))
        others = []
        for d in range(1, 1 << len(bits)):
            code, peer = 0, row
            for i, bit in enumerate(bits):
                own = own_bit(bit)
                flip = d >> i & 1
                code = code + (1 - own if flip else own) * (1 << i)
                peer = peer + ((1 - 2 * own) * (1 << bit) if flip else 0)
            others.append((code, peer))
        return mine, others

    def send_part(q, stage, at, slot, size, split):
        groups, extras = parts[q]
        bits = groups[stage] if split else extras[stage]
        mine, others = members(bits)
        piece = size >> len(bits) if split else size
        keep = pl.multiple_of(base[q] + mine * piece if split else base[q], SUBLANES)
        width = starts[q + 1] - starts[q]
        sent = []
        for d, (code, peer) in enumerate(others):
            give = pl.multiple_of(base[q] + code * piece, SUBLANES) if split else keep
            copy = pltpu.make_async_remote_copy(
                src_ref=prod.at[pl.ds(give, piece), pl.ds(starts[q], width)],
                dst_ref=halves.at[q, pl.ds(at + d * piece, piece), pl.ds(0, width)],
                send_sem=red_send.at[q, slot + d], recv_sem=red_recv.at[q, slot + d],
                device_id=(peer, col), device_id_type=MESH)
            copy.start()
            sent.append((copy, at + d * piece))
        base[q] = keep
        return sent, keep, piece, width

    def send_stage(stage, at, slot, size, split, before):
        held = []
        for q in range(len(parts)):
            before(q)
            if split:
                marks[q].append(base[q])
            held.append(send_part(q, stage, at, slot, size, split))
        used, piece = len(held[0][0]), held[0][2]
        return held, at + used * piece, slot + used, piece

    def adder(held):
        def add_part(q):
            sent, keep, piece, width = held[q]
            for copy, _ in sent:
                copy.wait()
            spot = (pl.ds(keep, piece), slice(starts[q], starts[q + 1]))
            value = prod[spot]
            for _, at in sent:
                value = value + halves[q, at : at + piece, :width]
            prod[spot] = value

        return add_part

    def share_part(q, stage, slot, piece):
        _, others = members(parts[q][0][stage])
        keep = pl.multiple_of(base[q], SUBLANES)
        spot = total.at[pl.ds(keep, piece), pl.ds(starts[q], starts[q + 1] - starts[q])]
        sent = []
        for d, (_, peer) in enumerate(others):
            copy = pltpu.make_async_remote_copy(
                src_ref=spot, dst_ref=spot, send_sem=red_send.at[q, slot + d], recv_sem=red_recv.at[q, slot + d],
                device_id=(peer, col), device_id_type=MESH)
            copy.start()
            sent.append(copy)
        return sent

    marks = [[] for _ in parts]
    at, slot, size = 0, 0, PANEL
    held, at, slot, size = send_stage(0, at, slot, size, True, lambda q: products(starts[q], starts[q + 1]))

    for copy in gathers:
        copy.wait()
    summed = gram_in[0]
    for k in range(1, n):
        summed = summed + gram_in[k]
    gram_all[own_rows, :] = summed
    spreads = []
    for step in range(1, chunks):
        peer = row - own_chunk + lax.rem(own_chunk + step, chunks)
        copy = pltpu.make_async_remote_copy(
            src_ref=gram_all.at[own_rows], dst_ref=gram_all.at[own_rows],
            send_sem=gram_send.at[n + step], recv_sem=gram_recv.at[n + step],
            device_id=(peer, col), device_id_type=MESH)
        copy.start()
        spreads.append(copy)

    for stage in range(1, nstages):
        held, at, slot, size = send_stage(stage, at, slot, size, True, adder(held))
    for copy in spreads:
        copy.wait()
    turns = PANEL // SUBLANES
    mat, done = gram_all[...], 0

    def turn_by(mat, done, share):
        upto = min(turns, done + share)
        return (sweep_groups(mat, upto - done) if upto > done else mat), upto

    mat, done = turn_by(mat, done, 3)
    for stage in range(len(parts[0][1])):
        held, at, slot, size = send_stage(stage, at, slot, size, False, adder(held))
    last_add = adder(held)
    waiting = [[] for _ in parts]
    for stage in reversed(range(nstages)):
        for q in range(len(parts)):
            if stage == nstages - 1:
                last_add(q)
                spot = (pl.ds(pl.multiple_of(base[q], SUBLANES), size), slice(starts[q], starts[q + 1]))
                total[spot] = prod[spot]
            for copy in waiting[q]:
                copy.wait()
            waiting[q] = share_part(q, stage, slot, size)
            base[q] = marks[q][stage]
        slot += len(waiting[0])
        mat, done = turn_by(mat, done, turns if stage == 0 else 4)
        size <<= len(parts[0][0][stage])

    inverse[...] = -mat
    high, low, _ = pieces(dot_full(block_panel, -mat))
    left[...] = jnp.concatenate([high, high, low], axis=1)
    for q in range(len(parts)):
        for copy in waiting[q]:
            copy.wait()


def finish(front, left, inverse, total, rhs_t, updated, side_t, left_t, stage, sems):
    nrhs = rhs_t.shape[0]
    cols_dev = front.shape[1]
    tile = stage.shape[2]
    left = left[...]

    def product(right):
        top, rest, _ = pieces(right)
        return dot(left, jnp.concatenate([top, rest, top], axis=0), ((1,), (0,)))

    copies = []
    for t in range(stage.shape[0]):
        at = slice(t * tile, (t + 1) * tile)
        stage[t] = front[:, at] - product(total[:, at])
        copy = pltpu.make_async_copy(stage.at[t], updated.at[:, pl.ds(t * tile, tile)], sems.at[t])
        copy.start()
        copies.append(copy)
    sides = total[:, cols_dev:]
    side_t[...] = jnp.transpose(dot_full(inverse[...], sides))[:nrhs]
    left_t[...] = rhs_t[...] - jnp.transpose(product(sides))[:nrhs]
    for copy in copies:
        copy.wait()


def solution(mesh):
    n, ncols = mesh.shape["rows"], mesh.shape["cols"]

    def shards(parent_front, right_sides, child_values, block_owner, row_map, col_map):
        rows_dev, cols_dev = parent_front.shape
        child_rows, child_cols = child_values.shape
        nrhs = right_sides.shape[1]
        side_width = -(-nrhs // LANES) * LANES
        width = cols_dev + side_width
        starts, parts, _ = plan(n, width)
        nparts = len(parts)
        widest = max(starts[q + 1] - starts[q] for q in range(nparts))
        landing_rows, slots = slots_of(n)
        block = child_rows // n
        chunks = min(n, PANEL // SUBLANES)
        vmem = pl.BlockSpec(memory_space=pltpu.VMEM)
        dma = pltpu.SemaphoreType.DMA
        hbm = pl.BlockSpec(memory_space=pltpu.HBM)
        rhs_t = right_sides.T
        operands = (block_owner, parent_front, rhs_t, child_values, row_map.reshape(1, -1), col_map.reshape(1, -1))
        front, left, inverse, total = pl.pallas_call(
            functools.partial(kernel, n, ncols),
            out_shape=(
                pltpu.VMEM((rows_dev, cols_dev), f32),
                pltpu.VMEM((rows_dev, 3 * PANEL), bf16),
                pltpu.VMEM((PANEL, PANEL), f32),
                pltpu.VMEM((PANEL, width), f32),
            ),
            in_specs=[hbm] * 6,
            out_specs=(vmem, vmem, vmem, vmem),
            scratch_shapes=[
                pltpu.VMEM((rows_dev, PANEL), f32),
                pltpu.SMEM(block_owner.shape, jnp.int32),
                pltpu.VMEM((nrhs, rows_dev), f32),
                pltpu.VMEM((1, child_rows), jnp.int32),
                pltpu.VMEM((1, child_cols), jnp.int32),
                pltpu.VMEM((child_rows, child_cols), f32),
                pltpu.VMEM((n, block, child_cols + LANES), f32),
                pltpu.VMEM((n, block, child_cols + LANES), f32),
                pltpu.VMEM((child_rows, child_cols + LANES), f32),
                pltpu.VMEM((cols_dev, child_cols), bf16),
                pltpu.VMEM((rows_dev, side_width), f32),
                pltpu.VMEM((PANEL, width), f32),
                pltpu.VMEM((nparts, landing_rows, widest), f32),
                pltpu.VMEM((PANEL, PANEL), f32),
                pltpu.VMEM((n, PANEL // chunks, PANEL), f32),
                pltpu.VMEM((PANEL, PANEL), f32),
                dma((6,)),
                dma((n,)),
                dma((n,)),
                dma((max(ncols - 1, 1),)),
                dma,
                dma((n + chunks,)),
                dma((n + chunks,)),
                dma((nparts, 2 * slots)),
                dma((nparts, 2 * slots)),
            ],
            compiler_params=pltpu.CompilerParams(collective_id=0, has_side_effects=True, vmem_limit_bytes=VMEM_LIMIT),
        )(*[pltpu.with_memory_space_constraint(value, pltpu.HBM) for value in operands])
        tile = min(TILE, cols_dev)
        updated, side_t, left_t = pl.pallas_call(
            finish,
            out_shape=(
                jax.ShapeDtypeStruct((rows_dev, cols_dev), f32),
                jax.ShapeDtypeStruct((nrhs, PANEL), f32),
                jax.ShapeDtypeStruct((nrhs, rows_dev), f32),
            ),
            in_specs=[vmem] * 5,
            out_specs=(hbm, vmem, vmem),
            scratch_shapes=[
                pltpu.VMEM((cols_dev // tile, rows_dev, tile), f32),
                dma((cols_dev // tile,)),
            ],
            compiler_params=pltpu.CompilerParams(vmem_limit_bytes=VMEM_LIMIT),
        )(front, left, inverse, total, rhs_t)
        return updated, side_t.T, left_t.T

    in_specs = (
        P("rows", "cols"),
        P("rows", None),
        P("rows", "cols"),
        P("rows"),
        P("rows"),
        P("cols"),
    )
    out_specs = (P("rows", "cols"), P(), P("rows", None))
    return jax.shard_map(shards, mesh=mesh, in_specs=in_specs, out_specs=out_specs, check_vma=False)
```

```python
import functools

import jax
import jax.numpy as jnp
from jax import lax
from jax.experimental import pallas as pl
from jax.experimental.pallas import tpu as pltpu
from jax.sharding import PartitionSpec as P

PANEL = 128
LANES = 128
SUBLANES = 8
TILE = 256
NPARTS = 3
SHARES = (6, 6, 4)
VMEM_LIMIT = 33521664
MESH = pl.DeviceIdType.MESH
f32 = jnp.float32
bf16 = jnp.bfloat16


def pieces(value):
    first = value.astype(bf16)
    rest = value - first.astype(f32)
    second = rest.astype(bf16)
    third = (rest - second.astype(f32)).astype(bf16)
    return first, second, third


def dot(left, right, dims, precision=None):
    return lax.dot_general(left, right, (dims, ((), ())), precision=precision, preferred_element_type=f32)


def dot_full(left, right, dims=((1,), (0,))):
    return dot(left, right, dims, lax.Precision.HIGHEST)


def inverse_pair(a, b, d):
    ia = 1.0 / a
    ratio = b * ia
    i11 = 1.0 / (d - b * ratio)
    i01 = -ratio * i11
    return ia - ratio * i01, i01, i11


def sweep_four(mat, k, lane):
    cols = [mat[:, k + j : k + j + 1] for j in range(4)]
    rows = [mat[k + j : k + j + 1, :] for j in range(4)]
    d = [[jnp.broadcast_to(mat[k + i : k + i + 1, k + j : k + j + 1], (1, mat.shape[1])) for j in range(i + 1)] for i in range(4)]
    a00, a01, a11 = inverse_pair(d[0][0], d[1][0], d[1][1])
    l20, l21 = d[2][0] * a00 + d[2][1] * a01, d[2][0] * a01 + d[2][1] * a11
    l30, l31 = d[3][0] * a00 + d[3][1] * a01, d[3][0] * a01 + d[3][1] * a11
    s22 = d[2][2] - (l20 * d[2][0] + l21 * d[2][1])
    s32 = d[3][2] - (l30 * d[2][0] + l31 * d[2][1])
    s33 = d[3][3] - (l30 * d[3][0] + l31 * d[3][1])
    e22, e32, e33 = inverse_pair(s22, s32, s33)
    e20, e21 = -(e22 * l20 + e32 * l30), -(e22 * l21 + e32 * l31)
    e30, e31 = -(e32 * l20 + e33 * l30), -(e32 * l21 + e33 * l31)
    e00 = a00 - (l20 * e20 + l30 * e30)
    e10 = a01 - (l21 * e20 + l31 * e30)
    e11 = a11 - (l21 * e21 + l31 * e31)
    e = [[e00, e10, e20, e30], [e10, e11, e21, e31], [e20, e21, e22, e32], [e30, e31, e32, e33]]
    lane_row = lane[:1]
    tops = []
    for i in range(4):
        top = (e[i][0] * rows[0] + e[i][1] * rows[1]) + (e[i][2] * rows[2] + e[i][3] * rows[3])
        for j in range(4):
            top = jnp.where(lane_row == k + j, -e[i][j], top)
        tops.append(top)
    out = jnp.where((lane >= k) & (lane < k + 4), 0.0, mat)
    out = out - ((cols[0] * tops[0] + cols[1] * tops[1]) + (cols[2] * tops[2] + cols[3] * tops[3]))
    head = out[:SUBLANES]
    sub = lax.broadcasted_iota(jnp.int32, head.shape, 0)
    for j in range(4):
        head = jnp.where(sub == k + j, tops[j], head)
    return jnp.concatenate([head, out[SUBLANES:]], axis=0)


def sweep_groups(mat, count):
    size = mat.shape[0]
    lane = lax.broadcasted_iota(jnp.int32, mat.shape, 1)

    def group(_, mat):
        for k in range(0, SUBLANES, 4):
            mat = sweep_four(mat, k, lane)
        mat = jnp.concatenate([mat[SUBLANES:], mat[:SUBLANES]], axis=0)
        return pltpu.roll(mat, size - SUBLANES, 1)

    return lax.fori_loop(0, count, group, mat)


def flipped(index, code):
    for bit in range(code.bit_length()):
        if code >> bit & 1:
            index = index + (1 - 2 * ((index // (1 << bit)) % 2)) * (1 << bit)
    return index


def plan(n, width):
    levels = n.bit_length() - 1
    halving = min(levels, (PANEL // SUBLANES).bit_length() - 1)
    norders = min(3, levels)
    tiles = width // LANES
    nparts = min(NPARTS, tiles)
    sizes = [tiles // nparts + (q < tiles % nparts) for q in range(nparts)]
    starts = [LANES * sum(sizes[:q]) for q in range(nparts + 1)]
    orders = [[(q + t) % norders for t in range(norders)] + list(range(norders, levels)) for q in range(nparts)]
    single = max(halving - 2, 0)
    cuts = [(t, t + 1) for t in range(single)] + [(single, halving)]
    parts = [([order[a:b] for a, b in cuts], [[bit] for bit in order[halving:]]) for order in orders]
    return starts, parts, halving


def landing_of(n):
    levels = n.bit_length() - 1
    halving = min(levels, (PANEL // SUBLANES).bit_length() - 1)
    single = max(halving - 2, 0)
    rows, size = 0, PANEL
    for bits in [1] * single + [halving - single]:
        size >>= bits
        rows += ((1 << bits) - 1) * size
    return rows + (levels - halving) * SUBLANES, single + 1, levels - halving


def landed(ref, send_sem, recv_sem, peer):
    return pltpu.make_async_remote_copy(
        src_ref=ref, dst_ref=ref, send_sem=send_sem, recv_sem=recv_sem, device_id=peer, device_id_type=MESH)


def kernel(n, ncols, owner_hbm, parent, rhs_hbm, child_hbm, row_map_hbm, col_map_hbm,
           front, left, inverse, total, side, panel, owner, rhs_t, row_map, col_map, child,
           lead_out, lead_in, tail_out, tail_in, flat, hot, prod, halves, gram, gram_in, gram_all,
           in_sem, lead_sem, tail_sem, pan_sem, gram_sem, side_sem, send_sem, recv_sem, extra_sem):
    row, col = lax.axis_index("rows"), lax.axis_index("cols")
    rows_dev, cols_dev = front.shape
    child_rows, child_cols = child.shape
    nrhs = rhs_t.shape[0]
    block = child_rows // n
    spare = cols_dev - child_cols
    other = (flipped(row, 1), col)
    first_loads = [
        pltpu.make_async_copy(source, target, in_sem.at[k])
        for k, (source, target) in enumerate([(owner_hbm, owner), (row_map_hbm, row_map), (child_hbm, child)])
    ]
    later_loads = [
        pltpu.make_async_copy(source, target, in_sem.at[3 + k])
        for k, (source, target) in enumerate([(col_map_hbm, col_map), (rhs_hbm, rhs_t), (parent, front)])
    ]
    for load in first_loads + later_loads:
        load.start()

    barrier = pltpu.get_barrier_semaphore()
    for code in reversed(range(1, n)):
        pl.semaphore_signal(barrier, inc=1, device_id=(flipped(row, code), col), device_id_type=MESH)
    for step in range(1, ncols):
        pl.semaphore_signal(barrier, inc=1, device_id=(row, lax.rem(col + step, ncols)), device_id_type=MESH)

    for load in first_loads:
        load.wait()
    source = lax.broadcasted_iota(jnp.int32, (1, child_rows), 1)
    target = jnp.zeros((1, child_rows), jnp.int32)
    for k in range(n):
        target = jnp.where(source // block == k, owner[k] * block + source % block, target)
    place = lax.broadcasted_iota(jnp.int32, (child_rows, child_rows), 0) == target
    place_f = jnp.where(place, 1.0, 0.0).astype(f32)
    landing = jnp.sum(place_f * row_map[...].astype(f32), axis=1, keepdims=True)
    place_b = place_f.astype(bf16)
    one, two, three = pieces(child[...])
    ordered = dot(place_b, one, ((1,), (0,))) + dot(place_b, two, ((1,), (0,))) + dot(place_b, three, ((1,), (0,)))
    slot_of = lax.broadcasted_iota(jnp.int32, (child_rows, LANES), 0)
    lane_of = lax.broadcasted_iota(jnp.int32, (child_rows, LANES), 1)
    spots = jnp.where(lane_of == row * block + slot_of % block, landing, 0.0)
    pick = lax.broadcasted_iota(jnp.int32, (n, child_rows), 0) == lax.broadcasted_iota(jnp.int32, (n, child_rows), 1) // block
    heads = dot_full(jnp.where(pick, 1.0, 0.0).astype(f32), spots)
    for k in range(n):
        lead_out[k, :block] = ordered[k * block : (k + 1) * block, :LANES]
        lead_out[k, block : block + 1] = heads[k : k + 1]
        tail_out[k] = ordered[k * block : (k + 1) * block, LANES:]

    pl.semaphore_wait(barrier, n - 1 + ncols - 1)

    for source_ref, target_ref, sem in ((lead_out, lead_in, lead_sem), (tail_out, tail_in, tail_sem)):
        for code in reversed(range(1, n)):
            peer = flipped(row, code)
            pltpu.make_async_remote_copy(
                src_ref=source_ref.at[peer], dst_ref=target_ref.at[row], send_sem=sem.at[0], recv_sem=sem.at[1],
                device_id=(peer, col), device_id_type=MESH).start()
    lead_in[row] = lead_out[row]
    tail_in[row] = tail_out[row]

    for load in later_loads:
        load.wait()
    cols_at = lax.broadcasted_iota(jnp.int32, hot.shape, 0)
    hot[...] = jnp.where(cols_at == col_map[...], 1.0, 0.0).astype(f32).astype(bf16)
    padded = jnp.concatenate([rhs_t[...], jnp.zeros((LANES - nrhs, rows_dev), f32)], axis=0)
    sides = jnp.transpose(padded)

    lead_all = landed(lead_in.at[pl.ds(0, n - 1)], lead_sem.at[0], lead_sem.at[1], other)
    lead_all.wait_recv()
    heads = lead_in[0, block : block + 1]
    for k in range(1, n):
        heads = heads + lead_in[k, block : block + 1]
    for k in range(n):
        flat[k * block : (k + 1) * block, :LANES] = lead_in[k, :block]
    spot = lax.broadcasted_iota(jnp.int32, (rows_dev, child_rows), 0) == heads[:, :child_rows].astype(jnp.int32)
    spot_b = jnp.where(spot, 1.0, 0.0).astype(f32).astype(bf16)
    spot3 = jnp.concatenate([spot_b] * 3, axis=1)

    def assemble(vals, first, last):
        low = max(0, first - spare) // LANES * LANES
        high = min(child_cols, last)
        spread = dot(vals[:, low:high], hot[first:last, low:high], ((1,), (1,)))
        front[:, first:last] = front[:, first:last] + dot(spot3, spread.astype(bf16), ((1,), (0,)))

    lead_vals = jnp.concatenate(pieces(flat[:, :LANES]), axis=0)
    assemble(lead_vals, 0, PANEL)
    pan_copies = [
        pltpu.make_async_remote_copy(
            src_ref=front.at[:, pl.ds(0, PANEL)], dst_ref=panel, send_sem=pan_sem.at[1 + step], recv_sem=pan_sem.at[0],
            device_id=(row, step), device_id_type=MESH)
        for step in range(1, ncols)
    ]

    @pl.when(col == 0)
    def _():
        for copy in pan_copies:
            copy.start()
        panel[...] = front[:, :PANEL]

    @pl.when(col != 0)
    def _():
        pan_copies[0].wait_recv()

    block_panel = panel[...]
    turned = jnp.transpose(block_panel)
    gram[...] = dot_full(turned, block_panel)

    chunks = min(n, PANEL // SUBLANES)
    chunk = PANEL // chunks
    own_chunk = lax.rem(row, chunks)
    own_rows = pl.ds(pl.multiple_of(own_chunk * chunk, SUBLANES), chunk)
    for code in reversed(range(1, n)):
        peer = flipped(row, code)
        start = pl.multiple_of(lax.rem(peer, chunks) * chunk, SUBLANES)
        pltpu.make_async_remote_copy(
            src_ref=gram.at[pl.ds(start, chunk)], dst_ref=gram_in.at[row],
            send_sem=gram_sem.at[0], recv_sem=gram_sem.at[1], device_id=(peer, col), device_id_type=MESH).start()
    gram_in[row] = gram[own_rows, :]

    tail_all = landed(tail_in.at[pl.ds(0, n - 1)], tail_sem.at[0], tail_sem.at[1], other)
    tail_all.wait_recv()
    for k in range(n):
        flat[k * block : (k + 1) * block, LANES:] = tail_in[k]
    vals = jnp.concatenate([lead_vals, jnp.concatenate(pieces(flat[:, LANES:]), axis=0)], axis=1)
    first = PANEL
    while first < cols_dev:
        last = min(cols_dev, (first // TILE + 1) * TILE)
        assemble(vals, first, last)
        first = last

    high, low, _ = pieces(turned)
    turned3 = jnp.concatenate([high, high, low], axis=1)
    opening = jnp.where(col == 0, sides, front[:, :PANEL])

    def products(first, last):
        def product(right):
            top, rest, _ = pieces(right)
            return dot(turned3, jnp.concatenate([top, rest, top], axis=0), ((1,), (0,)))

        if first == 0:
            prod[:, :PANEL] = product(opening)
            first = PANEL
        if last > first:
            prod[:, first:last] = product(front[:, first:last])

    starts, parts, halving = plan(n, prod.shape[1])
    base = [row * 0] * len(parts)
    nstages = len(parts[0][0])

    def own_bit(bit):
        return (row // (1 << bit)) % 2

    def members(bits):
        mine = sum(own_bit(bit) * (1 << i) for i, bit in enumerate(bits))
        others = []
        for d in reversed(range(1, 1 << len(bits))):
            code, peer = 0, row
            for i, bit in enumerate(bits):
                own = own_bit(bit)
                flip = d >> i & 1
                code = code + (1 - own if flip else own) * (1 << i)
                peer = peer + ((1 - 2 * own) * (1 << bit) if flip else 0)
            others.append((code, peer))
        return mine, others

    def send_part(q, stage, at, size, split):
        groups, extras = parts[q]
        bits = groups[stage] if split else extras[stage]
        mine, others = members(bits)
        piece = size >> len(bits) if split else size
        keep = pl.multiple_of(base[q] + mine * piece if split else base[q], SUBLANES)
        width = starts[q + 1] - starts[q]
        send, recv = (send_sem.at[0], recv_sem.at[q, stage]) if split else (extra_sem.at[0, q, stage], extra_sem.at[1, q, stage])
        for d, (code, peer) in enumerate(others):
            give = pl.multiple_of(base[q] + code * piece, SUBLANES) if split else keep
            pltpu.make_async_remote_copy(
                src_ref=prod.at[pl.ds(give, piece), pl.ds(starts[q], width)],
                dst_ref=halves.at[q, pl.ds(at + d * piece, piece), pl.ds(0, width)],
                send_sem=send, recv_sem=recv, device_id=(peer, col), device_id_type=MESH).start()
        base[q] = keep
        return len(others), at, send, recv, keep, piece, width

    def send_stage(stage, at, size, split, before):
        held = []
        for q in range(len(parts)):
            before(q)
            if split:
                marks[q].append(base[q])
            held.append(send_part(q, stage, at, size, split))
        used, piece = held[0][0], held[0][5]
        return (held, split), at + used * piece, piece

    def adder(state):
        held, split = state

        def add_part(q):
            used, at, send, recv, keep, piece, width = held[q]
            whole = landed(halves.at[q, pl.ds(at, used * piece), pl.ds(0, width)], send, recv, other)
            whole.wait_recv()
            if not split:
                whole.wait_send()
            spot = (pl.ds(keep, piece), slice(starts[q], starts[q + 1]))
            value = prod[spot]
            for d in range(used):
                value = value + halves[q, at + d * piece : at + (d + 1) * piece, :width]
            prod[spot] = value

        return add_part

    def share_part(q, stage, piece):
        _, others = members(parts[q][0][stage])
        keep = pl.multiple_of(base[q], SUBLANES)
        columns = pl.ds(starts[q], starts[q + 1] - starts[q])
        spot = total.at[pl.ds(keep, piece), columns]
        recv = recv_sem.at[q, nstages + stage]
        for _, peer in others:
            pltpu.make_async_remote_copy(
                src_ref=spot, dst_ref=spot, send_sem=send_sem.at[1], recv_sem=recv,
                device_id=(peer, col), device_id_type=MESH).start()
        return landed(total.at[pl.ds(0, len(others) * piece), columns], send_sem.at[1], recv, other)

    marks = [[] for _ in parts]
    at, size = 0, PANEL
    held, at, size = send_stage(0, at, size, True, lambda q: products(starts[q], starts[q + 1]))

    gathered = landed(gram_in.at[pl.ds(0, n - 1)], gram_sem.at[0], gram_sem.at[1], other)
    gathered.wait_recv()
    summed = gram_in[0]
    for k in range(1, n):
        summed = summed + gram_in[k]
    gram_all[own_rows, :] = summed
    for code in reversed(range(1, chunks)):
        peer = row - own_chunk + flipped(own_chunk, code)
        pltpu.make_async_remote_copy(
            src_ref=gram_all.at[own_rows], dst_ref=gram_all.at[own_rows],
            send_sem=gram_sem.at[2], recv_sem=gram_sem.at[3], device_id=(peer, col), device_id_type=MESH).start()

    for stage in range(1, nstages):
        held, at, size = send_stage(stage, at, size, True, adder(held))
    spread_all = landed(gram_all.at[pl.ds(0, (chunks - 1) * chunk)], gram_sem.at[2], gram_sem.at[3], other)
    spread_all.wait_recv()
    turns = PANEL // SUBLANES
    mat, done = gram_all[...], 0

    def turn_by(mat, done, share):
        upto = min(turns, done + share)
        return (sweep_groups(mat, upto - done) if upto > done else mat), upto

    mat, done = turn_by(mat, done, SHARES[0])
    for stage in range(len(parts[0][1])):
        held, at, size = send_stage(stage, at, size, False, adder(held))
    last_add = adder(held)
    waiting = [None for _ in parts]
    for stage in reversed(range(nstages)):
        for q in range(len(parts)):
            if stage == nstages - 1:
                last_add(q)
                spot = (pl.ds(pl.multiple_of(base[q], SUBLANES), size), slice(starts[q], starts[q + 1]))
                total[spot] = prod[spot]
            else:
                waiting[q].wait_recv()
            waiting[q] = share_part(q, stage, size)
            base[q] = marks[q][stage]
        mat, done = turn_by(mat, done, turns if stage == 0 else SHARES[1 + nstages - 1 - stage])
        size <<= len(parts[0][0][stage])

    inverse[...] = -mat
    high, low, _ = pieces(dot_full(block_panel, -mat))
    left[...] = jnp.concatenate([high, high, low], axis=1)
    for q in range(len(parts)):
        waiting[q].wait_recv()
        if q == 0:
            side_copies = [
                pltpu.make_async_remote_copy(
                    src_ref=side, dst_ref=side, send_sem=side_sem.at[1 + step], recv_sem=side_sem.at[0],
                    device_id=(row, step), device_id_type=MESH)
                for step in range(1, ncols)
            ]

            @pl.when(col == 0)
            def _():
                side[...] = total[:, :PANEL]
                for copy in side_copies:
                    copy.start()

    lead_all.wait_send()
    tail_all.wait_send()
    gathered.wait_send()
    spread_all.wait_send()
    for k in range(2):
        landed(total.at[pl.ds(0, PANEL - (PANEL >> halving))], send_sem.at[k], send_sem.at[k], other).wait_send()

    @pl.when(col == 0)
    def _():
        for copy in pan_copies + side_copies:
            copy.wait_send()
        total[:, :PANEL] = gram_all[...]

    @pl.when(col != 0)
    def _():
        side_copies[0].wait_recv()


def finish(front, left, inverse, total, side, rhs_t, updated, side_t, left_t, stage, sems):
    nrhs = rhs_t.shape[0]
    tile = stage.shape[2]
    left = left[...]

    def product(right):
        top, rest, _ = pieces(right)
        return dot(left, jnp.concatenate([top, rest, top], axis=0), ((1,), (0,)))

    copies = []
    for t in range(stage.shape[0]):
        at = slice(t * tile, (t + 1) * tile)
        stage[t] = front[:, at] - product(total[:, at])
        copy = pltpu.make_async_copy(stage.at[t], updated.at[:, pl.ds(t * tile, tile)], sems.at[t])
        copy.start()
        copies.append(copy)
    sides = side[...]
    side_t[...] = jnp.transpose(dot_full(inverse[...], sides))[:nrhs]
    left_t[...] = rhs_t[...] - jnp.transpose(product(sides))[:nrhs]
    for copy in copies:
        copy.wait()


def solution(mesh):
    n, ncols = mesh.shape["rows"], mesh.shape["cols"]

    def shards(parent_front, right_sides, child_values, block_owner, row_map, col_map):
        rows_dev, cols_dev = parent_front.shape
        child_rows, child_cols = child_values.shape
        nrhs = right_sides.shape[1]
        starts, parts, _ = plan(n, cols_dev)
        nparts = len(parts)
        widest = max(starts[q + 1] - starts[q] for q in range(nparts))
        landing_rows, nstages, nextra = landing_of(n)
        block = child_rows // n
        chunks = min(n, PANEL // SUBLANES)
        vmem = pl.BlockSpec(memory_space=pltpu.VMEM)
        dma = pltpu.SemaphoreType.DMA
        hbm = pl.BlockSpec(memory_space=pltpu.HBM)
        rhs_t = right_sides.T
        operands = (block_owner, parent_front, rhs_t, child_values, row_map.reshape(1, -1), col_map.reshape(1, -1))
        front, left, inverse, total, side = pl.pallas_call(
            functools.partial(kernel, n, ncols),
            out_shape=(
                pltpu.VMEM((rows_dev, cols_dev), f32),
                pltpu.VMEM((rows_dev, 3 * PANEL), bf16),
                pltpu.VMEM((PANEL, PANEL), f32),
                pltpu.VMEM((PANEL, cols_dev), f32),
                pltpu.VMEM((PANEL, LANES), f32),
            ),
            in_specs=[hbm] * 6,
            out_specs=(vmem,) * 5,
            scratch_shapes=[
                pltpu.VMEM((rows_dev, PANEL), f32),
                pltpu.SMEM(block_owner.shape, jnp.int32),
                pltpu.VMEM((nrhs, rows_dev), f32),
                pltpu.VMEM((1, child_rows), jnp.int32),
                pltpu.VMEM((1, child_cols), jnp.int32),
                pltpu.VMEM((child_rows, child_cols), f32),
                pltpu.VMEM((n, block + 1, LANES), f32),
                pltpu.VMEM((n, block + 1, LANES), f32),
                pltpu.VMEM((n, block, child_cols - LANES), f32),
                pltpu.VMEM((n, block, child_cols - LANES), f32),
                pltpu.VMEM((child_rows, child_cols), f32),
                pltpu.VMEM((cols_dev, child_cols), bf16),
                pltpu.VMEM((PANEL, cols_dev), f32),
                pltpu.VMEM((nparts, landing_rows, widest), f32),
                pltpu.VMEM((PANEL, PANEL), f32),
                pltpu.VMEM((n, PANEL // chunks, PANEL), f32),
                pltpu.VMEM((PANEL, PANEL), f32),
                dma((6,)),
                dma((2,)),
                dma((2,)),
                dma((ncols + 1,)),
                dma((4,)),
                dma((ncols + 1,)),
                dma((2,)),
                dma((nparts, 2 * nstages)),
                dma((2, nparts, max(nextra, 1))),
            ],
            compiler_params=pltpu.CompilerParams(collective_id=0, has_side_effects=True, vmem_limit_bytes=VMEM_LIMIT),
        )(*[pltpu.with_memory_space_constraint(value, pltpu.HBM) for value in operands])
        tile = min(TILE, cols_dev)
        updated, side_t, left_t = pl.pallas_call(
            finish,
            out_shape=(
                jax.ShapeDtypeStruct((rows_dev, cols_dev), f32),
                jax.ShapeDtypeStruct((nrhs, PANEL), f32),
                jax.ShapeDtypeStruct((nrhs, rows_dev), f32),
            ),
            in_specs=[vmem] * 6,
            out_specs=(hbm, vmem, vmem),
            scratch_shapes=[
                pltpu.VMEM((cols_dev // tile, rows_dev, tile), f32),
                dma((cols_dev // tile,)),
            ],
            compiler_params=pltpu.CompilerParams(vmem_limit_bytes=VMEM_LIMIT),
        )(front, left, inverse, total, side, rhs_t)
        return updated, side_t.T, left_t.T

    in_specs = (
        P("rows", "cols"),
        P("rows", None),
        P("rows", "cols"),
        P("rows"),
        P("rows"),
        P("cols"),
    )
    out_specs = (P("rows", "cols"), P(), P("rows", None))
    return jax.shard_map(shards, mesh=mesh, in_specs=in_specs, out_specs=out_specs, check_vma=False)
```

```python
import functools

import jax
import jax.numpy as jnp
from jax import lax
from jax.experimental import pallas as pl
from jax.experimental.pallas import tpu as pltpu
from jax.sharding import PartitionSpec as P

PANEL = 128
LANES = 128
SUBLANES = 8
TILE = 256
NPARTS = 6
SHARES = (6, 6, 4)
VMEM_LIMIT = 33521664
MESH = pl.DeviceIdType.MESH
f32 = jnp.float32
bf16 = jnp.bfloat16


def pieces(value):
    first = value.astype(bf16)
    rest = value - first.astype(f32)
    second = rest.astype(bf16)
    third = (rest - second.astype(f32)).astype(bf16)
    return first, second, third


def dot(left, right, dims, precision=None):
    return lax.dot_general(left, right, (dims, ((), ())), precision=precision, preferred_element_type=f32)


def dot_full(left, right, dims=((1,), (0,))):
    return dot(left, right, dims, lax.Precision.HIGHEST)


def inverse_pair(a, b, d):
    ia = 1.0 / a
    ratio = b * ia
    i11 = 1.0 / (d - b * ratio)
    i01 = -ratio * i11
    return ia - ratio * i01, i01, i11


def sweep_four(mat, k, lane):
    cols = [mat[:, k + j : k + j + 1] for j in range(4)]
    rows = [mat[k + j : k + j + 1, :] for j in range(4)]
    d = [[jnp.broadcast_to(mat[k + i : k + i + 1, k + j : k + j + 1], (1, mat.shape[1])) for j in range(i + 1)] for i in range(4)]
    a00, a01, a11 = inverse_pair(d[0][0], d[1][0], d[1][1])
    l20, l21 = d[2][0] * a00 + d[2][1] * a01, d[2][0] * a01 + d[2][1] * a11
    l30, l31 = d[3][0] * a00 + d[3][1] * a01, d[3][0] * a01 + d[3][1] * a11
    s22 = d[2][2] - (l20 * d[2][0] + l21 * d[2][1])
    s32 = d[3][2] - (l30 * d[2][0] + l31 * d[2][1])
    s33 = d[3][3] - (l30 * d[3][0] + l31 * d[3][1])
    e22, e32, e33 = inverse_pair(s22, s32, s33)
    e20, e21 = -(e22 * l20 + e32 * l30), -(e22 * l21 + e32 * l31)
    e30, e31 = -(e32 * l20 + e33 * l30), -(e32 * l21 + e33 * l31)
    e00 = a00 - (l20 * e20 + l30 * e30)
    e10 = a01 - (l21 * e20 + l31 * e30)
    e11 = a11 - (l21 * e21 + l31 * e31)
    e = [[e00, e10, e20, e30], [e10, e11, e21, e31], [e20, e21, e22, e32], [e30, e31, e32, e33]]
    lane_row = lane[:1]
    tops = []
    for i in range(4):
        top = (e[i][0] * rows[0] + e[i][1] * rows[1]) + (e[i][2] * rows[2] + e[i][3] * rows[3])
        for j in range(4):
            top = jnp.where(lane_row == k + j, -e[i][j], top)
        tops.append(top)
    out = jnp.where((lane >= k) & (lane < k + 4), 0.0, mat)
    out = out - ((cols[0] * tops[0] + cols[1] * tops[1]) + (cols[2] * tops[2] + cols[3] * tops[3]))
    head = out[:SUBLANES]
    sub = lax.broadcasted_iota(jnp.int32, head.shape, 0)
    for j in range(4):
        head = jnp.where(sub == k + j, tops[j], head)
    return jnp.concatenate([head, out[SUBLANES:]], axis=0)


def sweep_groups(mat, count):
    size = mat.shape[0]
    lane = lax.broadcasted_iota(jnp.int32, mat.shape, 1)

    def group(_, mat):
        for k in range(0, SUBLANES, 4):
            mat = sweep_four(mat, k, lane)
        mat = jnp.concatenate([mat[SUBLANES:], mat[:SUBLANES]], axis=0)
        return pltpu.roll(mat, size - SUBLANES, 1)

    return lax.fori_loop(0, count, group, mat)


def flipped(index, code):
    for bit in range(code.bit_length()):
        if code >> bit & 1:
            index = index + (1 - 2 * ((index // (1 << bit)) % 2)) * (1 << bit)
    return index


def plan(n, width):
    levels = n.bit_length() - 1
    halving = min(levels, (PANEL // SUBLANES).bit_length() - 1)
    norders = min(3, levels)
    tiles = width // LANES
    nparts = min(NPARTS, tiles)
    sizes = [tiles // nparts + (q < tiles % nparts) for q in range(nparts)]
    starts = [LANES * sum(sizes[:q]) for q in range(nparts + 1)]
    orders = [[(q + t) % norders for t in range(norders)] + list(range(norders, levels)) for q in range(nparts)]
    single = max(halving - 2, 0)
    cuts = [(t, t + 1) for t in range(single)] + [(single, halving)]
    parts = [([order[a:b] for a, b in cuts], [[bit] for bit in order[halving:]]) for order in orders]
    return starts, parts, halving


def landing_of(n):
    levels = n.bit_length() - 1
    halving = min(levels, (PANEL // SUBLANES).bit_length() - 1)
    single = max(halving - 2, 0)
    rows, size = 0, PANEL
    for bits in [1] * single + [halving - single]:
        size >>= bits
        rows += ((1 << bits) - 1) * size
    return rows + (levels - halving) * SUBLANES, single + 1, levels - halving


def landed(ref, send_sem, recv_sem, peer):
    return pltpu.make_async_remote_copy(
        src_ref=ref, dst_ref=ref, send_sem=send_sem, recv_sem=recv_sem, device_id=peer, device_id_type=MESH)


def kernel(n, ncols, owner_hbm, parent, rhs_hbm, child_hbm, row_map_hbm, col_map_hbm,
           front, left, inverse, total, side, panel, owner, rhs_t, row_map, col_map, child,
           lead_out, lead_in, tail_out, tail_in, flat, stacked, spread_at, turned3, hot, prod, halves, gram, gram_in, gram_all,
           in_sem, lead_sem, tail_sem, pan_sem, gram_sem, side_sem, send_sem, recv_sem, extra_sem):
    row, col = lax.axis_index("rows"), lax.axis_index("cols")
    rows_dev, cols_dev = front.shape
    child_rows, child_cols = child.shape
    nrhs = rhs_t.shape[0]
    block = child_rows // n
    spare = cols_dev - child_cols
    other = (flipped(row, 1), col)
    first_loads = [
        pltpu.make_async_copy(source, target, in_sem.at[k])
        for k, (source, target) in enumerate([(owner_hbm, owner), (row_map_hbm, row_map), (child_hbm, child)])
    ]
    later_loads = [
        pltpu.make_async_copy(source, target, in_sem.at[3 + k])
        for k, (source, target) in enumerate([(col_map_hbm, col_map), (rhs_hbm, rhs_t), (parent, front)])
    ]
    for load in first_loads + later_loads:
        load.start()

    barrier = pltpu.get_barrier_semaphore()
    for code in reversed(range(1, n)):
        pl.semaphore_signal(barrier, inc=1, device_id=(flipped(row, code), col), device_id_type=MESH)
    for step in range(1, ncols):
        pl.semaphore_signal(barrier, inc=1, device_id=(row, lax.rem(col + step, ncols)), device_id_type=MESH)

    for load in first_loads:
        load.wait()
    source = lax.broadcasted_iota(jnp.int32, (1, child_rows), 1)
    target = jnp.zeros((1, child_rows), jnp.int32)
    for k in range(n):
        target = jnp.where(source // block == k, owner[k] * block + source % block, target)
    place = lax.broadcasted_iota(jnp.int32, (child_rows, child_rows), 0) == target
    place_f = jnp.where(place, 1.0, 0.0).astype(f32)
    landing = jnp.sum(place_f * row_map[...].astype(f32), axis=1, keepdims=True)
    place_b = place_f.astype(bf16)
    one, two, three = pieces(child[...])
    ordered = dot(place_b, one, ((1,), (0,))) + dot(place_b, two, ((1,), (0,))) + dot(place_b, three, ((1,), (0,)))
    slot_of = lax.broadcasted_iota(jnp.int32, (child_rows, LANES), 0)
    lane_of = lax.broadcasted_iota(jnp.int32, (child_rows, LANES), 1)
    spots = jnp.where(lane_of == row * block + slot_of % block, landing, 0.0)
    pick = lax.broadcasted_iota(jnp.int32, (n, child_rows), 0) == lax.broadcasted_iota(jnp.int32, (n, child_rows), 1) // block
    heads = dot_full(jnp.where(pick, 1.0, 0.0).astype(f32), spots)
    for k in range(n):
        lead_out[k, :block] = ordered[k * block : (k + 1) * block, :LANES]
        lead_out[k, block : block + 1] = heads[k : k + 1]
        tail_out[k] = ordered[k * block : (k + 1) * block, LANES:]

    pl.semaphore_wait(barrier, n - 1 + ncols - 1)

    for source_ref, target_ref, sem in ((lead_out, lead_in, lead_sem), (tail_out, tail_in, tail_sem)):
        for code in reversed(range(1, n)):
            peer = flipped(row, code)
            pltpu.make_async_remote_copy(
                src_ref=source_ref.at[peer], dst_ref=target_ref.at[row], send_sem=sem.at[0], recv_sem=sem.at[1],
                device_id=(peer, col), device_id_type=MESH).start()
    lead_in[row] = lead_out[row]
    tail_in[row] = tail_out[row]

    for load in later_loads:
        load.wait()
    cols_at = lax.broadcasted_iota(jnp.int32, hot.shape, 0)
    hot[...] = jnp.where(cols_at == col_map[...], 1.0, 0.0).astype(f32).astype(bf16)
    padded = jnp.concatenate([rhs_t[...], jnp.zeros((LANES - nrhs, rows_dev), f32)], axis=0)
    sides = jnp.transpose(padded)

    lead_all = landed(lead_in.at[pl.ds(0, n - 1)], lead_sem.at[0], lead_sem.at[1], other)
    lead_all.wait_recv()
    heads = lead_in[0, block : block + 1]
    for k in range(1, n):
        heads = heads + lead_in[k, block : block + 1]
    for k in range(n):
        flat[k * block : (k + 1) * block, :LANES] = lead_in[k, :block]
    spot = lax.broadcasted_iota(jnp.int32, (rows_dev, child_rows), 0) == heads[:, :child_rows].astype(jnp.int32)
    spot_b = jnp.where(spot, 1.0, 0.0).astype(f32).astype(bf16)
    spread_at[...] = jnp.concatenate([spot_b] * 3, axis=1)

    def assemble(vals, first, last):
        low = max(0, first - spare) // LANES * LANES
        high = min(child_cols, last)
        spread = dot(vals[:, low:high], hot[first:last, low:high], ((1,), (1,)))
        front[:, first:last] = front[:, first:last] + dot(spread_at[...], spread.astype(bf16), ((1,), (0,)))

    lead_vals = jnp.concatenate(pieces(flat[:, :LANES]), axis=0)
    assemble(lead_vals, 0, PANEL)
    pan_copies = [
        pltpu.make_async_remote_copy(
            src_ref=front.at[:, pl.ds(0, PANEL)], dst_ref=panel, send_sem=pan_sem.at[1 + step], recv_sem=pan_sem.at[0],
            device_id=(row, step), device_id_type=MESH)
        for step in range(1, ncols)
    ]

    @pl.when(col == 0)
    def _():
        for copy in pan_copies:
            copy.start()
        panel[...] = front[:, :PANEL]

    chunks = min(n, PANEL // SUBLANES)
    chunk = PANEL // chunks
    own_chunk = lax.rem(row, chunks)
    own_rows = pl.ds(pl.multiple_of(own_chunk * chunk, SUBLANES), chunk)

    def gram_step():
        turned = jnp.transpose(panel[...])
        gram[...] = dot_full(turned, panel[...])
        for code in reversed(range(1, n)):
            peer = flipped(row, code)
            start = pl.multiple_of(lax.rem(peer, chunks) * chunk, SUBLANES)
            pltpu.make_async_remote_copy(
                src_ref=gram.at[pl.ds(start, chunk)], dst_ref=gram_in.at[row],
                send_sem=gram_sem.at[0], recv_sem=gram_sem.at[1], device_id=(peer, col), device_id_type=MESH).start()
        gram_in[row] = gram[own_rows, :]
        high, low, _ = pieces(turned)
        turned3[...] = jnp.concatenate([high, high, low], axis=1)

    pl.when(col == 0)(gram_step)

    tail_all = landed(tail_in.at[pl.ds(0, n - 1)], tail_sem.at[0], tail_sem.at[1], other)
    tail_all.wait_recv()
    for k in range(n):
        flat[k * block : (k + 1) * block, LANES:] = tail_in[k]
    tail_vals = jnp.concatenate(pieces(flat[:, LANES:]), axis=0)
    stacked[...] = jnp.concatenate([lead_vals, tail_vals], axis=1)

    def assemble_block(first):
        last = min(cols_dev, first + TILE)
        assemble(stacked, max(first, PANEL), last)

    @pl.when(col != 0)
    def _():
        for first in range(0, cols_dev, TILE):
            assemble_block(first)
        pan_copies[0].wait_recv()
        gram_step()

    block_panel = panel[...]

    def product(right):
        top, rest, _ = pieces(right)
        return dot(turned3[...], jnp.concatenate([top, rest, top], axis=0), ((1,), (0,)))

    ready = [0]

    def products(last):
        while ready[0] < last:
            first = ready[0]
            upto = min(cols_dev, first + TILE)

            @pl.when(col == 0)
            def _():
                assemble_block(first)

            right = front[:, first:upto]
            if first == 0:
                right = jnp.concatenate([jnp.where(col == 0, sides, right[:, :PANEL]), right[:, PANEL:]], axis=1)
            prod[:, first:upto] = product(right)
            ready[0] = upto

    starts, parts, halving = plan(n, prod.shape[1])
    base = [row * 0] * len(parts)
    nstages = len(parts[0][0])

    def own_bit(bit):
        return (row // (1 << bit)) % 2

    def members(bits):
        mine = sum(own_bit(bit) * (1 << i) for i, bit in enumerate(bits))
        others = []
        for d in reversed(range(1, 1 << len(bits))):
            code, peer = 0, row
            for i, bit in enumerate(bits):
                own = own_bit(bit)
                flip = d >> i & 1
                code = code + (1 - own if flip else own) * (1 << i)
                peer = peer + ((1 - 2 * own) * (1 << bit) if flip else 0)
            others.append((code, peer))
        return mine, others

    def send_part(q, stage, at, size, split):
        groups, extras = parts[q]
        bits = groups[stage] if split else extras[stage]
        mine, others = members(bits)
        piece = size >> len(bits) if split else size
        keep = pl.multiple_of(base[q] + mine * piece if split else base[q], SUBLANES)
        width = starts[q + 1] - starts[q]
        send, recv = (send_sem.at[0], recv_sem.at[q, stage]) if split else (extra_sem.at[0, q, stage], extra_sem.at[1, q, stage])
        for d, (code, peer) in enumerate(others):
            give = pl.multiple_of(base[q] + code * piece, SUBLANES) if split else keep
            pltpu.make_async_remote_copy(
                src_ref=prod.at[pl.ds(give, piece), pl.ds(starts[q], width)],
                dst_ref=halves.at[q, pl.ds(at + d * piece, piece), pl.ds(0, width)],
                send_sem=send, recv_sem=recv, device_id=(peer, col), device_id_type=MESH).start()
        base[q] = keep
        return len(others), at, send, recv, keep, piece, width

    def send_stage(stage, at, size, split, before):
        held = []
        for q in range(len(parts)):
            before(q)
            if split:
                marks[q].append(base[q])
            held.append(send_part(q, stage, at, size, split))
        used, piece = held[0][0], held[0][5]
        return (held, split), at + used * piece, piece

    def adder(state):
        held, split = state

        def add_part(q):
            used, at, send, recv, keep, piece, width = held[q]
            whole = landed(halves.at[q, pl.ds(at, used * piece), pl.ds(0, width)], send, recv, other)
            whole.wait_recv()
            if not split:
                whole.wait_send()
            spot = (pl.ds(keep, piece), slice(starts[q], starts[q + 1]))
            value = prod[spot]
            for d in range(used):
                value = value + halves[q, at + d * piece : at + (d + 1) * piece, :width]
            prod[spot] = value

        return add_part

    def share_part(q, stage, piece):
        _, others = members(parts[q][0][stage])
        keep = pl.multiple_of(base[q], SUBLANES)
        columns = pl.ds(starts[q], starts[q + 1] - starts[q])
        spot = total.at[pl.ds(keep, piece), columns]
        recv = recv_sem.at[q, nstages + stage]
        for _, peer in others:
            pltpu.make_async_remote_copy(
                src_ref=spot, dst_ref=spot, send_sem=send_sem.at[1], recv_sem=recv,
                device_id=(peer, col), device_id_type=MESH).start()
        return landed(total.at[pl.ds(0, len(others) * piece), columns], send_sem.at[1], recv, other)

    marks = [[] for _ in parts]
    at, size = 0, PANEL
    held, at, size = send_stage(0, at, size, True, lambda q: products(starts[q + 1]))

    gathered = landed(gram_in.at[pl.ds(0, n - 1)], gram_sem.at[0], gram_sem.at[1], other)
    gathered.wait_recv()
    summed = gram_in[0]
    for k in range(1, n):
        summed = summed + gram_in[k]
    gram_all[own_rows, :] = summed
    for code in reversed(range(1, chunks)):
        peer = row - own_chunk + flipped(own_chunk, code)
        pltpu.make_async_remote_copy(
            src_ref=gram_all.at[own_rows], dst_ref=gram_all.at[own_rows],
            send_sem=gram_sem.at[2], recv_sem=gram_sem.at[3], device_id=(peer, col), device_id_type=MESH).start()

    for stage in range(1, nstages):
        held, at, size = send_stage(stage, at, size, True, adder(held))
    spread_all = landed(gram_all.at[pl.ds(0, (chunks - 1) * chunk)], gram_sem.at[2], gram_sem.at[3], other)
    spread_all.wait_recv()
    turns = PANEL // SUBLANES
    mat, done = gram_all[...], 0

    def turn_by(mat, done, share):
        upto = min(turns, done + share)
        return (sweep_groups(mat, upto - done) if upto > done else mat), upto

    mat, done = turn_by(mat, done, SHARES[0])
    for stage in range(len(parts[0][1])):
        held, at, size = send_stage(stage, at, size, False, adder(held))
    last_add = adder(held)
    waiting = [None for _ in parts]
    for stage in reversed(range(nstages)):
        for q in range(len(parts)):
            if stage == nstages - 1:
                last_add(q)
                spot = (pl.ds(pl.multiple_of(base[q], SUBLANES), size), slice(starts[q], starts[q + 1]))
                total[spot] = prod[spot]
            else:
                waiting[q].wait_recv()
            waiting[q] = share_part(q, stage, size)
            base[q] = marks[q][stage]
        mat, done = turn_by(mat, done, turns if stage == 0 else SHARES[1 + nstages - 1 - stage])
        size <<= len(parts[0][0][stage])

    inverse[...] = -mat
    high, low, _ = pieces(dot_full(block_panel, -mat))
    left[...] = jnp.concatenate([high, high, low], axis=1)
    for q in range(len(parts)):
        waiting[q].wait_recv()
        if q == 0:
            side_copies = [
                pltpu.make_async_remote_copy(
                    src_ref=side, dst_ref=side, send_sem=side_sem.at[1 + step], recv_sem=side_sem.at[0],
                    device_id=(row, step), device_id_type=MESH)
                for step in range(1, ncols)
            ]

            @pl.when(col == 0)
            def _():
                side[...] = total[:, :PANEL]
                for copy in side_copies:
                    copy.start()

    lead_all.wait_send()
    tail_all.wait_send()
    gathered.wait_send()
    spread_all.wait_send()
    for k in range(2):
        landed(total.at[pl.ds(0, PANEL - (PANEL >> halving))], send_sem.at[k], send_sem.at[k], other).wait_send()

    @pl.when(col == 0)
    def _():
        for copy in pan_copies + side_copies:
            copy.wait_send()
        total[:, :PANEL] = gram_all[...]

    @pl.when(col != 0)
    def _():
        side_copies[0].wait_recv()


def finish(front, left, inverse, total, side, rhs_t, updated, side_t, left_t, stage, sems):
    nrhs = rhs_t.shape[0]
    tile = stage.shape[2]
    left = left[...]

    def product(right):
        top, rest, _ = pieces(right)
        return dot(left, jnp.concatenate([top, rest, top], axis=0), ((1,), (0,)))

    copies = []
    for t in range(stage.shape[0]):
        at = slice(t * tile, (t + 1) * tile)
        stage[t] = front[:, at] - product(total[:, at])
        copy = pltpu.make_async_copy(stage.at[t], updated.at[:, pl.ds(t * tile, tile)], sems.at[t])
        copy.start()
        copies.append(copy)
    sides = side[...]
    side_t[...] = jnp.transpose(dot_full(inverse[...], sides))[:nrhs]
    left_t[...] = rhs_t[...] - jnp.transpose(product(sides))[:nrhs]
    for copy in copies:
        copy.wait()


def solution(mesh):
    n, ncols = mesh.shape["rows"], mesh.shape["cols"]

    def shards(parent_front, right_sides, child_values, block_owner, row_map, col_map):
        rows_dev, cols_dev = parent_front.shape
        child_rows, child_cols = child_values.shape
        nrhs = right_sides.shape[1]
        starts, parts, _ = plan(n, cols_dev)
        nparts = len(parts)
        widest = max(starts[q + 1] - starts[q] for q in range(nparts))
        landing_rows, nstages, nextra = landing_of(n)
        block = child_rows // n
        chunks = min(n, PANEL // SUBLANES)
        vmem = pl.BlockSpec(memory_space=pltpu.VMEM)
        dma = pltpu.SemaphoreType.DMA
        hbm = pl.BlockSpec(memory_space=pltpu.HBM)
        rhs_t = right_sides.T
        operands = (block_owner, parent_front, rhs_t, child_values, row_map.reshape(1, -1), col_map.reshape(1, -1))
        front, left, inverse, total, side = pl.pallas_call(
            functools.partial(kernel, n, ncols),
            out_shape=(
                pltpu.VMEM((rows_dev, cols_dev), f32),
                pltpu.VMEM((rows_dev, 3 * PANEL), bf16),
                pltpu.VMEM((PANEL, PANEL), f32),
                pltpu.VMEM((PANEL, cols_dev), f32),
                pltpu.VMEM((PANEL, LANES), f32),
            ),
            in_specs=[hbm] * 6,
            out_specs=(vmem,) * 5,
            scratch_shapes=[
                pltpu.VMEM((rows_dev, PANEL), f32),
                pltpu.SMEM(block_owner.shape, jnp.int32),
                pltpu.VMEM((nrhs, rows_dev), f32),
                pltpu.VMEM((1, child_rows), jnp.int32),
                pltpu.VMEM((1, child_cols), jnp.int32),
                pltpu.VMEM((child_rows, child_cols), f32),
                pltpu.VMEM((n, block + 1, LANES), f32),
                pltpu.VMEM((n, block + 1, LANES), f32),
                pltpu.VMEM((n, block, child_cols - LANES), f32),
                pltpu.VMEM((n, block, child_cols - LANES), f32),
                pltpu.VMEM((child_rows, child_cols), f32),
                pltpu.VMEM((3 * child_rows, child_cols), bf16),
                pltpu.VMEM((rows_dev, 3 * child_rows), bf16),
                pltpu.VMEM((PANEL, 3 * rows_dev), bf16),
                pltpu.VMEM((cols_dev, child_cols), bf16),
                pltpu.VMEM((PANEL, cols_dev), f32),
                pltpu.VMEM((nparts, landing_rows, widest), f32),
                pltpu.VMEM((PANEL, PANEL), f32),
                pltpu.VMEM((n, PANEL // chunks, PANEL), f32),
                pltpu.VMEM((PANEL, PANEL), f32),
                dma((6,)),
                dma((2,)),
                dma((2,)),
                dma((ncols + 1,)),
                dma((4,)),
                dma((ncols + 1,)),
                dma((2,)),
                dma((nparts, 2 * nstages)),
                dma((2, nparts, max(nextra, 1))),
            ],
            compiler_params=pltpu.CompilerParams(collective_id=0, has_side_effects=True, vmem_limit_bytes=VMEM_LIMIT),
        )(*[pltpu.with_memory_space_constraint(value, pltpu.HBM) for value in operands])
        tile = min(TILE, cols_dev)
        updated, side_t, left_t = pl.pallas_call(
            finish,
            out_shape=(
                jax.ShapeDtypeStruct((rows_dev, cols_dev), f32),
                jax.ShapeDtypeStruct((nrhs, PANEL), f32),
                jax.ShapeDtypeStruct((nrhs, rows_dev), f32),
            ),
            in_specs=[vmem] * 6,
            out_specs=(hbm, vmem, vmem),
            scratch_shapes=[
                pltpu.VMEM((cols_dev // tile, rows_dev, tile), f32),
                dma((cols_dev // tile,)),
            ],
            compiler_params=pltpu.CompilerParams(vmem_limit_bytes=VMEM_LIMIT),
        )(front, left, inverse, total, side, rhs_t)
        return updated, side_t.T, left_t.T

    in_specs = (
        P("rows", "cols"),
        P("rows", None),
        P("rows", "cols"),
        P("rows"),
        P("rows"),
        P("cols"),
    )
    out_specs = (P("rows", "cols"), P(), P("rows", None))
    return jax.shard_map(shards, mesh=mesh, in_specs=in_specs, out_specs=out_specs, check_vma=False)
```

```python
import functools

import jax
import jax.numpy as jnp
from jax import lax
from jax.experimental import pallas as pl
from jax.experimental.pallas import tpu as pltpu
from jax.sharding import PartitionSpec as P

PANEL = 128
LANES = 128
SUBLANES = 8
TILE = 256
NPARTS = 6
SHARES = (6, 6, 4)
VMEM_LIMIT = 33521664
MESH = pl.DeviceIdType.MESH
f32 = jnp.float32
bf16 = jnp.bfloat16


def pieces(value):
    first = value.astype(bf16)
    rest = value - first.astype(f32)
    second = rest.astype(bf16)
    third = (rest - second.astype(f32)).astype(bf16)
    return first, second, third


def dot(left, right, dims, precision=None):
    return lax.dot_general(left, right, (dims, ((), ())), precision=precision, preferred_element_type=f32)


def dot_full(left, right, dims=((1,), (0,))):
    return dot(left, right, dims, lax.Precision.HIGHEST)


def inverse_pair(a, b, d):
    ia = 1.0 / a
    ratio = b * ia
    i11 = 1.0 / (d - b * ratio)
    i01 = -ratio * i11
    return ia - ratio * i01, i01, i11


def sweep_four(mat, k, lane):
    cols = [mat[:, k + j : k + j + 1] for j in range(4)]
    rows = [mat[k + j : k + j + 1, :] for j in range(4)]
    d = [[jnp.broadcast_to(mat[k + i : k + i + 1, k + j : k + j + 1], (1, mat.shape[1])) for j in range(i + 1)] for i in range(4)]
    a00, a01, a11 = inverse_pair(d[0][0], d[1][0], d[1][1])
    l20, l21 = d[2][0] * a00 + d[2][1] * a01, d[2][0] * a01 + d[2][1] * a11
    l30, l31 = d[3][0] * a00 + d[3][1] * a01, d[3][0] * a01 + d[3][1] * a11
    s22 = d[2][2] - (l20 * d[2][0] + l21 * d[2][1])
    s32 = d[3][2] - (l30 * d[2][0] + l31 * d[2][1])
    s33 = d[3][3] - (l30 * d[3][0] + l31 * d[3][1])
    e22, e32, e33 = inverse_pair(s22, s32, s33)
    e20, e21 = -(e22 * l20 + e32 * l30), -(e22 * l21 + e32 * l31)
    e30, e31 = -(e32 * l20 + e33 * l30), -(e32 * l21 + e33 * l31)
    e00 = a00 - (l20 * e20 + l30 * e30)
    e10 = a01 - (l21 * e20 + l31 * e30)
    e11 = a11 - (l21 * e21 + l31 * e31)
    e = [[e00, e10, e20, e30], [e10, e11, e21, e31], [e20, e21, e22, e32], [e30, e31, e32, e33]]
    lane_row = lane[:1]
    tops = []
    for i in range(4):
        top = (e[i][0] * rows[0] + e[i][1] * rows[1]) + (e[i][2] * rows[2] + e[i][3] * rows[3])
        for j in range(4):
            top = jnp.where(lane_row == k + j, -e[i][j], top)
        tops.append(top)
    out = jnp.where((lane >= k) & (lane < k + 4), 0.0, mat)
    out = out - ((cols[0] * tops[0] + cols[1] * tops[1]) + (cols[2] * tops[2] + cols[3] * tops[3]))
    head = out[:SUBLANES]
    sub = lax.broadcasted_iota(jnp.int32, head.shape, 0)
    for j in range(4):
        head = jnp.where(sub == k + j, tops[j], head)
    return jnp.concatenate([head, out[SUBLANES:]], axis=0)


def sweep_groups(mat, count):
    size = mat.shape[0]
    lane = lax.broadcasted_iota(jnp.int32, mat.shape, 1)

    def group(_, mat):
        for k in range(0, SUBLANES, 4):
            mat = sweep_four(mat, k, lane)
        mat = jnp.concatenate([mat[SUBLANES:], mat[:SUBLANES]], axis=0)
        return pltpu.roll(mat, size - SUBLANES, 1)

    return lax.fori_loop(0, count, group, mat)


def flipped(index, code):
    moves = [((1 << bit) - 2 * (1 << bit) * ((index // (1 << bit)) % 2)) for bit in range(code.bit_length())]
    for bit, move in enumerate(moves):
        if code >> bit & 1:
            index = index + move
    return index


def plan(n, width):
    levels = n.bit_length() - 1
    halving = min(levels, (PANEL // SUBLANES).bit_length() - 1)
    norders = min(3, levels)
    tiles = width // LANES
    nparts = min(NPARTS, tiles)
    sizes = [tiles // nparts + (q < tiles % nparts) for q in range(nparts)]
    starts = [LANES * sum(sizes[:q]) for q in range(nparts + 1)]
    orders = [[(q + t) % norders for t in range(norders)] + list(range(norders, levels)) for q in range(nparts)]
    single = max(halving - 2, 0)
    cuts = [(t, t + 1) for t in range(single)] + [(single, halving)]
    parts = [([order[a:b] for a, b in cuts], [[bit] for bit in order[halving:]]) for order in orders]
    return starts, parts, halving


def landing_of(n):
    levels = n.bit_length() - 1
    halving = min(levels, (PANEL // SUBLANES).bit_length() - 1)
    single = max(halving - 2, 0)
    rows, size = 0, PANEL
    for bits in [1] * single + [halving - single]:
        size >>= bits
        rows += ((1 << bits) - 1) * size
    return rows + (levels - halving) * SUBLANES, single + 1, levels - halving


def landed(ref, send_sem, recv_sem, peer):
    return pltpu.make_async_remote_copy(
        src_ref=ref, dst_ref=ref, send_sem=send_sem, recv_sem=recv_sem, device_id=peer, device_id_type=MESH)


def kernel(n, ncols, owner_hbm, parent, rhs_hbm, child_hbm, row_map_hbm, col_map_hbm,
           front, left, inverse, total, side, panel, owner, rhs_t, row_map, col_map, child,
           lead_out, lead_in, tail_out, tail_in, flat, stacked, spread_at, turned3, hot, prod, halves, gram, gram_in, gram_all,
           in_sem, lead_sem, tail_sem, pan_sem, gram_sem, side_sem, send_sem, recv_sem, extra_sem):
    row, col = lax.axis_index("rows"), lax.axis_index("cols")
    rows_dev, cols_dev = front.shape
    child_rows, child_cols = child.shape
    nrhs = rhs_t.shape[0]
    block = child_rows // n
    spare = cols_dev - child_cols
    other = (flipped(row, 1), col)
    first_loads = [
        pltpu.make_async_copy(source, target, in_sem.at[k])
        for k, (source, target) in enumerate([(owner_hbm, owner), (row_map_hbm, row_map), (child_hbm, child)])
    ]
    later_loads = [
        pltpu.make_async_copy(source, target, in_sem.at[3 + k])
        for k, (source, target) in enumerate([(col_map_hbm, col_map), (rhs_hbm, rhs_t), (parent, front)])
    ]
    for load in first_loads + later_loads:
        load.start()

    barrier = pltpu.get_barrier_semaphore()
    for code in reversed(range(1, n)):
        pl.semaphore_signal(barrier, inc=1, device_id=(flipped(row, code), col), device_id_type=MESH)
    for step in range(1, ncols):
        pl.semaphore_signal(barrier, inc=1, device_id=(row, lax.rem(col + step, ncols)), device_id_type=MESH)

    for load in first_loads:
        load.wait()
    source = lax.broadcasted_iota(jnp.int32, (1, child_rows), 1)
    target = jnp.zeros((1, child_rows), jnp.int32)
    for k in range(n):
        target = jnp.where(source // block == k, owner[k] * block + source % block, target)
    place = lax.broadcasted_iota(jnp.int32, (child_rows, child_rows), 0) == target
    place_f = jnp.where(place, 1.0, 0.0).astype(f32)
    landing = jnp.sum(place_f * row_map[...].astype(f32), axis=1, keepdims=True)
    place_b = place_f.astype(bf16)
    one, two, three = pieces(child[...])
    ordered = dot(place_b, one, ((1,), (0,))) + dot(place_b, two, ((1,), (0,))) + dot(place_b, three, ((1,), (0,)))
    slot_of = lax.broadcasted_iota(jnp.int32, (child_rows, LANES), 0)
    lane_of = lax.broadcasted_iota(jnp.int32, (child_rows, LANES), 1)
    spots = jnp.where(lane_of == row * block + slot_of % block, landing, 0.0)
    pick = lax.broadcasted_iota(jnp.int32, (n, child_rows), 0) == lax.broadcasted_iota(jnp.int32, (n, child_rows), 1) // block
    heads = dot_full(jnp.where(pick, 1.0, 0.0).astype(f32), spots)
    for k in range(n):
        lead_out[k, :block] = ordered[k * block : (k + 1) * block, :LANES]
        lead_out[k, block : block + 1] = heads[k : k + 1]
        tail_out[k] = ordered[k * block : (k + 1) * block, LANES:]

    pl.semaphore_wait(barrier, n - 1 + ncols - 1)

    for source_ref, target_ref, sem in ((lead_out, lead_in, lead_sem), (tail_out, tail_in, tail_sem)):
        for code in reversed(range(1, n)):
            peer = flipped(row, code)
            pltpu.make_async_remote_copy(
                src_ref=source_ref.at[peer], dst_ref=target_ref.at[row], send_sem=sem.at[0], recv_sem=sem.at[1],
                device_id=(peer, col), device_id_type=MESH).start()
    lead_in[row] = lead_out[row]
    tail_in[row] = tail_out[row]

    for load in later_loads:
        load.wait()
    cols_at = lax.broadcasted_iota(jnp.int32, hot.shape, 0)
    hot[...] = jnp.where(cols_at == col_map[...], 1.0, 0.0).astype(f32).astype(bf16)
    padded = jnp.concatenate([rhs_t[...], jnp.zeros((LANES - nrhs, rows_dev), f32)], axis=0)
    sides = jnp.transpose(padded)

    lead_all = landed(lead_in.at[pl.ds(0, n - 1)], lead_sem.at[0], lead_sem.at[1], other)
    lead_all.wait_recv()
    heads = lead_in[0, block : block + 1]
    for k in range(1, n):
        heads = heads + lead_in[k, block : block + 1]
    for k in range(n):
        flat[k * block : (k + 1) * block, :LANES] = lead_in[k, :block]
    spot = lax.broadcasted_iota(jnp.int32, (rows_dev, child_rows), 0) == heads[:, :child_rows].astype(jnp.int32)
    spot_b = jnp.where(spot, 1.0, 0.0).astype(f32).astype(bf16)
    spread_at[...] = jnp.concatenate([spot_b] * 3, axis=1)

    def assemble(vals, first, last):
        low = max(0, first - spare) // LANES * LANES
        high = min(child_cols, last)
        spread = dot(vals[:, low:high], hot[first:last, low:high], ((1,), (1,)))
        front[:, first:last] = front[:, first:last] + dot(spread_at[...], spread.astype(bf16), ((1,), (0,)))

    lead_vals = jnp.concatenate(pieces(flat[:, :LANES]), axis=0)
    assemble(lead_vals, 0, PANEL)
    pan_copies = [
        pltpu.make_async_remote_copy(
            src_ref=front.at[:, pl.ds(0, PANEL)], dst_ref=panel, send_sem=pan_sem.at[1 + step], recv_sem=pan_sem.at[0],
            device_id=(row, step), device_id_type=MESH)
        for step in range(1, ncols)
    ]

    @pl.when(col == 0)
    def _():
        for copy in pan_copies:
            copy.start()
        panel[...] = front[:, :PANEL]

    chunks = min(n, PANEL // SUBLANES)
    chunk = PANEL // chunks
    own_chunk = lax.rem(row, chunks)
    own_rows = pl.ds(pl.multiple_of(own_chunk * chunk, SUBLANES), chunk)

    def gram_step():
        turned = jnp.transpose(panel[...])
        gram[...] = dot_full(turned, panel[...])
        for code in reversed(range(1, n)):
            peer = flipped(row, code)
            start = pl.multiple_of(lax.rem(peer, chunks) * chunk, SUBLANES)
            pltpu.make_async_remote_copy(
                src_ref=gram.at[pl.ds(start, chunk)], dst_ref=gram_in.at[row],
                send_sem=gram_sem.at[0], recv_sem=gram_sem.at[1], device_id=(peer, col), device_id_type=MESH).start()
        gram_in[row] = gram[own_rows, :]
        high, low, _ = pieces(turned)
        turned3[...] = jnp.concatenate([high, high, low], axis=1)

    pl.when(col == 0)(gram_step)

    tail_all = landed(tail_in.at[pl.ds(0, n - 1)], tail_sem.at[0], tail_sem.at[1], other)
    tail_all.wait_recv()
    for k in range(n):
        flat[k * block : (k + 1) * block, LANES:] = tail_in[k]
    tail_vals = jnp.concatenate(pieces(flat[:, LANES:]), axis=0)
    stacked[...] = jnp.concatenate([lead_vals, tail_vals], axis=1)

    def assemble_block(first):
        last = min(cols_dev, first + TILE)
        assemble(stacked, max(first, PANEL), last)

    @pl.when(col != 0)
    def _():
        for first in range(0, cols_dev, TILE):
            assemble_block(first)
        pan_copies[0].wait_recv()
        gram_step()

    block_panel = panel[...]

    def product(right):
        top, rest, _ = pieces(right)
        return dot(turned3[...], jnp.concatenate([top, rest, top], axis=0), ((1,), (0,)))

    ready = [0]

    def products(last):
        while ready[0] < last:
            first = ready[0]
            upto = min(cols_dev, first + TILE)

            @pl.when(col == 0)
            def _():
                assemble_block(first)

            right = front[:, first:upto]
            if first == 0:
                right = jnp.concatenate([jnp.where(col == 0, sides, right[:, :PANEL]), right[:, PANEL:]], axis=1)
            prod[:, first:upto] = product(right)
            ready[0] = upto

    starts, parts, halving = plan(n, prod.shape[1])
    base = [row * 0] * len(parts)
    nstages = len(parts[0][0])

    def own_bit(bit):
        return (row // (1 << bit)) % 2

    def members(bits):
        mine = sum(own_bit(bit) * (1 << i) for i, bit in enumerate(bits))
        others = []
        for d in reversed(range(1, 1 << len(bits))):
            code, peer = 0, row
            for i, bit in enumerate(bits):
                own = own_bit(bit)
                flip = d >> i & 1
                code = code + (1 - own if flip else own) * (1 << i)
                peer = peer + ((1 - 2 * own) * (1 << bit) if flip else 0)
            others.append((code, peer))
        return mine, others

    def send_part(q, stage, at, size, split):
        groups, extras = parts[q]
        bits = groups[stage] if split else extras[stage]
        mine, others = members(bits)
        piece = size >> len(bits) if split else size
        keep = pl.multiple_of(base[q] + mine * piece if split else base[q], SUBLANES)
        width = starts[q + 1] - starts[q]
        send, recv = (send_sem.at[0], recv_sem.at[q, stage]) if split else (extra_sem.at[0, q, stage], extra_sem.at[1, q, stage])
        for d, (code, peer) in enumerate(others):
            give = pl.multiple_of(base[q] + code * piece, SUBLANES) if split else keep
            pltpu.make_async_remote_copy(
                src_ref=prod.at[pl.ds(give, piece), pl.ds(starts[q], width)],
                dst_ref=halves.at[q, pl.ds(at + d * piece, piece), pl.ds(0, width)],
                send_sem=send, recv_sem=recv, device_id=(peer, col), device_id_type=MESH).start()
        base[q] = keep
        return len(others), at, send, recv, keep, piece, width

    def send_stage(stage, at, size, split, before):
        held = []
        for q in range(len(parts)):
            before(q)
            if split:
                marks[q].append(base[q])
            held.append(send_part(q, stage, at, size, split))
        used, piece = held[0][0], held[0][5]
        return (held, split), at + used * piece, piece

    def adder(state):
        held, split = state

        def add_part(q):
            used, at, send, recv, keep, piece, width = held[q]
            whole = landed(halves.at[q, pl.ds(at, used * piece), pl.ds(0, width)], send, recv, other)
            whole.wait_recv()
            if not split:
                whole.wait_send()
            spot = (pl.ds(keep, piece), slice(starts[q], starts[q + 1]))
            value = prod[spot]
            for d in range(used):
                value = value + halves[q, at + d * piece : at + (d + 1) * piece, :width]
            prod[spot] = value

        return add_part

    def share_part(q, stage, piece):
        _, others = members(parts[q][0][stage])
        keep = pl.multiple_of(base[q], SUBLANES)
        columns = pl.ds(starts[q], starts[q + 1] - starts[q])
        spot = total.at[pl.ds(keep, piece), columns]
        recv = recv_sem.at[q, nstages + stage]
        for _, peer in others:
            pltpu.make_async_remote_copy(
                src_ref=spot, dst_ref=spot, send_sem=send_sem.at[1], recv_sem=recv,
                device_id=(peer, col), device_id_type=MESH).start()
        return landed(total.at[pl.ds(0, len(others) * piece), columns], send_sem.at[1], recv, other)

    marks = [[] for _ in parts]
    at, size = 0, PANEL
    held, at, size = send_stage(0, at, size, True, lambda q: products(starts[q + 1]))

    gathered = landed(gram_in.at[pl.ds(0, n - 1)], gram_sem.at[0], gram_sem.at[1], other)
    gathered.wait_recv()
    summed = gram_in[0]
    for k in range(1, n):
        summed = summed + gram_in[k]
    gram_all[own_rows, :] = summed
    for code in reversed(range(1, chunks)):
        peer = row - own_chunk + flipped(own_chunk, code)
        pltpu.make_async_remote_copy(
            src_ref=gram_all.at[own_rows], dst_ref=gram_all.at[own_rows],
            send_sem=gram_sem.at[2], recv_sem=gram_sem.at[3], device_id=(peer, col), device_id_type=MESH).start()

    for stage in range(1, nstages):
        held, at, size = send_stage(stage, at, size, True, adder(held))
    spread_all = landed(gram_all.at[pl.ds(0, (chunks - 1) * chunk)], gram_sem.at[2], gram_sem.at[3], other)
    spread_all.wait_recv()
    turns = PANEL // SUBLANES
    mat, done = gram_all[...], 0

    def turn_by(mat, done, share):
        upto = min(turns, done + share)
        return (sweep_groups(mat, upto - done) if upto > done else mat), upto

    mat, done = turn_by(mat, done, SHARES[0])
    for stage in range(len(parts[0][1])):
        held, at, size = send_stage(stage, at, size, False, adder(held))
    last_add = adder(held)
    waiting = [None for _ in parts]
    for stage in reversed(range(nstages)):
        for q in range(len(parts)):
            if stage == nstages - 1:
                last_add(q)
                spot = (pl.ds(pl.multiple_of(base[q], SUBLANES), size), slice(starts[q], starts[q + 1]))
                total[spot] = prod[spot]
            else:
                waiting[q].wait_recv()
            waiting[q] = share_part(q, stage, size)
            base[q] = marks[q][stage]
        mat, done = turn_by(mat, done, turns if stage == 0 else SHARES[1 + nstages - 1 - stage])
        size <<= len(parts[0][0][stage])

    inverse[...] = -mat
    high, low, _ = pieces(dot_full(block_panel, -mat))
    left[...] = jnp.concatenate([high, high, low], axis=1)
    for q in range(len(parts)):
        waiting[q].wait_recv()
        if q == 0:
            side_copies = [
                pltpu.make_async_remote_copy(
                    src_ref=side, dst_ref=side, send_sem=side_sem.at[1 + step], recv_sem=side_sem.at[0],
                    device_id=(row, step), device_id_type=MESH)
                for step in range(1, ncols)
            ]

            @pl.when(col == 0)
            def _():
                side[...] = total[:, :PANEL]
                for copy in side_copies:
                    copy.start()

    lead_all.wait_send()
    tail_all.wait_send()
    gathered.wait_send()
    spread_all.wait_send()
    for k in range(2):
        landed(total.at[pl.ds(0, PANEL - (PANEL >> halving))], send_sem.at[k], send_sem.at[k], other).wait_send()

    @pl.when(col == 0)
    def _():
        for copy in pan_copies + side_copies:
            copy.wait_send()
        total[:, :PANEL] = gram_all[...]

    @pl.when(col != 0)
    def _():
        side_copies[0].wait_recv()


def finish(front, left, inverse, total, side, rhs_t, updated, side_out, left_out, stage, side_t, left_t, sems):
    nrhs = rhs_t.shape[0]
    tile = stage.shape[2]
    count = stage.shape[0]
    left = left[...]

    def product(right):
        top, rest, _ = pieces(right)
        return dot(left, jnp.concatenate([top, rest, top], axis=0), ((1,), (0,)))

    copies = []
    for t in range(count):
        at = slice(t * tile, (t + 1) * tile)
        stage[t] = front[:, at] - product(total[:, at])
        copies.append(pltpu.make_async_copy(stage.at[t], updated.at[:, pl.ds(t * tile, tile)], sems.at[t]))
        copies[-1].start()
        if t == 0:
            sides = side[...]
            side_t[...] = jnp.transpose(dot_full(inverse[...], sides))[:nrhs]
            left_t[...] = rhs_t[...] - jnp.transpose(product(sides))[:nrhs]
            for k, (source, target) in enumerate([(side_t, side_out), (left_t, left_out)]):
                copies.append(pltpu.make_async_copy(source, target, sems.at[count + k]))
                copies[-1].start()
    for copy in copies:
        copy.wait()


def solution(mesh):
    n, ncols = mesh.shape["rows"], mesh.shape["cols"]

    def shards(parent_front, right_sides, child_values, block_owner, row_map, col_map):
        rows_dev, cols_dev = parent_front.shape
        child_rows, child_cols = child_values.shape
        nrhs = right_sides.shape[1]
        starts, parts, _ = plan(n, cols_dev)
        nparts = len(parts)
        widest = max(starts[q + 1] - starts[q] for q in range(nparts))
        landing_rows, nstages, nextra = landing_of(n)
        block = child_rows // n
        chunks = min(n, PANEL // SUBLANES)
        vmem = pl.BlockSpec(memory_space=pltpu.VMEM)
        dma = pltpu.SemaphoreType.DMA
        hbm = pl.BlockSpec(memory_space=pltpu.HBM)
        rhs_t = right_sides.T
        operands = (block_owner, parent_front, rhs_t, child_values, row_map.reshape(1, -1), col_map.reshape(1, -1))
        front, left, inverse, total, side = pl.pallas_call(
            functools.partial(kernel, n, ncols),
            out_shape=(
                pltpu.VMEM((rows_dev, cols_dev), f32),
                pltpu.VMEM((rows_dev, 3 * PANEL), bf16),
                pltpu.VMEM((PANEL, PANEL), f32),
                pltpu.VMEM((PANEL, cols_dev), f32),
                pltpu.VMEM((PANEL, LANES), f32),
            ),
            in_specs=[hbm] * 6,
            out_specs=(vmem,) * 5,
            scratch_shapes=[
                pltpu.VMEM((rows_dev, PANEL), f32),
                pltpu.SMEM(block_owner.shape, jnp.int32),
                pltpu.VMEM((nrhs, rows_dev), f32),
                pltpu.VMEM((1, child_rows), jnp.int32),
                pltpu.VMEM((1, child_cols), jnp.int32),
                pltpu.VMEM((child_rows, child_cols), f32),
                pltpu.VMEM((n, block + 1, LANES), f32),
                pltpu.VMEM((n, block + 1, LANES), f32),
                pltpu.VMEM((n, block, child_cols - LANES), f32),
                pltpu.VMEM((n, block, child_cols - LANES), f32),
                pltpu.VMEM((child_rows, child_cols), f32),
                pltpu.VMEM((3 * child_rows, child_cols), bf16),
                pltpu.VMEM((rows_dev, 3 * child_rows), bf16),
                pltpu.VMEM((PANEL, 3 * rows_dev), bf16),
                pltpu.VMEM((cols_dev, child_cols), bf16),
                pltpu.VMEM((PANEL, cols_dev), f32),
                pltpu.VMEM((nparts, landing_rows, widest), f32),
                pltpu.VMEM((PANEL, PANEL), f32),
                pltpu.VMEM((n, PANEL // chunks, PANEL), f32),
                pltpu.VMEM((PANEL, PANEL), f32),
                dma((6,)),
                dma((2,)),
                dma((2,)),
                dma((ncols + 1,)),
                dma((4,)),
                dma((ncols + 1,)),
                dma((2,)),
                dma((nparts, 2 * nstages)),
                dma((2, nparts, nextra) if nextra else (1,)),
            ],
            compiler_params=pltpu.CompilerParams(collective_id=0, has_side_effects=True, vmem_limit_bytes=VMEM_LIMIT),
        )(*[pltpu.with_memory_space_constraint(value, pltpu.HBM) for value in operands])
        tile = min(TILE, cols_dev)
        updated, side_t, left_t = pl.pallas_call(
            finish,
            out_shape=(
                jax.ShapeDtypeStruct((rows_dev, cols_dev), f32),
                jax.ShapeDtypeStruct((nrhs, PANEL), f32),
                jax.ShapeDtypeStruct((nrhs, rows_dev), f32),
            ),
            in_specs=[vmem] * 6,
            out_specs=(hbm, hbm, hbm),
            scratch_shapes=[
                pltpu.VMEM((cols_dev // tile, rows_dev, tile), f32),
                pltpu.VMEM((nrhs, PANEL), f32),
                pltpu.VMEM((nrhs, rows_dev), f32),
                dma((cols_dev // tile + 2,)),
            ],
            compiler_params=pltpu.CompilerParams(vmem_limit_bytes=VMEM_LIMIT),
        )(front, left, inverse, total, side, rhs_t)
        return updated, side_t.T, left_t.T

    in_specs = (
        P("rows", "cols"),
        P("rows", None),
        P("rows", "cols"),
        P("rows"),
        P("rows"),
        P("cols"),
    )
    out_specs = (P("rows", "cols"), P(), P("rows", None))
    return jax.shard_map(shards, mesh=mesh, in_specs=in_specs, out_specs=out_specs, check_vma=False)
```

```python
import functools

import jax
import jax.numpy as jnp
from jax import lax
from jax.experimental import pallas as pl
from jax.experimental.pallas import tpu as pltpu
from jax.sharding import PartitionSpec as P

PANEL = 128
LANES = 128
SUBLANES = 8
TILE = 256
NPARTS = 6
SHARES = (6, 6, 4)
VMEM_LIMIT = 33521664
MESH = pl.DeviceIdType.MESH
f32 = jnp.float32
bf16 = jnp.bfloat16


def pieces(value):
    first = value.astype(bf16)
    rest = value - first.astype(f32)
    second = rest.astype(bf16)
    third = (rest - second.astype(f32)).astype(bf16)
    return first, second, third


def dot(left, right, dims, precision=None):
    return lax.dot_general(left, right, (dims, ((), ())), precision=precision, preferred_element_type=f32)


def dot_full(left, right, dims=((1,), (0,))):
    return dot(left, right, dims, lax.Precision.HIGHEST)


def inverse_pair(a, b, d):
    ia = 1.0 / a
    ratio = b * ia
    i11 = 1.0 / (d - b * ratio)
    i01 = -ratio * i11
    return ia - ratio * i01, i01, i11


def sweep_four(mat, k, lane):
    cols = [mat[:, k + j : k + j + 1] for j in range(4)]
    rows = [mat[k + j : k + j + 1, :] for j in range(4)]
    d = [[jnp.broadcast_to(mat[k + i : k + i + 1, k + j : k + j + 1], (1, mat.shape[1])) for j in range(i + 1)] for i in range(4)]
    a00, a01, a11 = inverse_pair(d[0][0], d[1][0], d[1][1])
    l20, l21 = d[2][0] * a00 + d[2][1] * a01, d[2][0] * a01 + d[2][1] * a11
    l30, l31 = d[3][0] * a00 + d[3][1] * a01, d[3][0] * a01 + d[3][1] * a11
    s22 = d[2][2] - (l20 * d[2][0] + l21 * d[2][1])
    s32 = d[3][2] - (l30 * d[2][0] + l31 * d[2][1])
    s33 = d[3][3] - (l30 * d[3][0] + l31 * d[3][1])
    e22, e32, e33 = inverse_pair(s22, s32, s33)
    e20, e21 = -(e22 * l20 + e32 * l30), -(e22 * l21 + e32 * l31)
    e30, e31 = -(e32 * l20 + e33 * l30), -(e32 * l21 + e33 * l31)
    e00 = a00 - (l20 * e20 + l30 * e30)
    e10 = a01 - (l21 * e20 + l31 * e30)
    e11 = a11 - (l21 * e21 + l31 * e31)
    e = [[e00, e10, e20, e30], [e10, e11, e21, e31], [e20, e21, e22, e32], [e30, e31, e32, e33]]
    lane_row = lane[:1]
    tops = []
    for i in range(4):
        top = (e[i][0] * rows[0] + e[i][1] * rows[1]) + (e[i][2] * rows[2] + e[i][3] * rows[3])
        for j in range(4):
            top = jnp.where(lane_row == k + j, -e[i][j], top)
        tops.append(top)
    out = jnp.where((lane >= k) & (lane < k + 4), 0.0, mat)
    out = out - ((cols[0] * tops[0] + cols[1] * tops[1]) + (cols[2] * tops[2] + cols[3] * tops[3]))
    head = out[:SUBLANES]
    sub = lax.broadcasted_iota(jnp.int32, head.shape, 0)
    for j in range(4):
        head = jnp.where(sub == k + j, tops[j], head)
    return jnp.concatenate([head, out[SUBLANES:]], axis=0)


def sweep_groups(mat, count):
    size = mat.shape[0]
    lane = lax.broadcasted_iota(jnp.int32, mat.shape, 1)

    def group(_, mat):
        for k in range(0, SUBLANES, 4):
            mat = sweep_four(mat, k, lane)
        mat = jnp.concatenate([mat[SUBLANES:], mat[:SUBLANES]], axis=0)
        return pltpu.roll(mat, size - SUBLANES, 1)

    return lax.fori_loop(0, count, group, mat)


def flipped(index, code):
    moves = [((1 << bit) - 2 * (1 << bit) * ((index // (1 << bit)) % 2)) for bit in range(code.bit_length())]
    for bit, move in enumerate(moves):
        if code >> bit & 1:
            index = index + move
    return index


def plan(n, width):
    levels = n.bit_length() - 1
    halving = min(levels, (PANEL // SUBLANES).bit_length() - 1)
    norders = min(3, levels)
    tiles = width // LANES
    nparts = min(NPARTS, tiles)
    sizes = [tiles // nparts + (q < tiles % nparts) for q in range(nparts)]
    starts = [LANES * sum(sizes[:q]) for q in range(nparts + 1)]
    orders = [[(q + t) % norders for t in range(norders)] + list(range(norders, levels)) for q in range(nparts)]
    single = max(halving - 2, 0)
    cuts = [(t, t + 1) for t in range(single)] + [(single, halving)]
    parts = [([order[a:b] for a, b in cuts], [[bit] for bit in order[halving:]]) for order in orders]
    return starts, parts, halving


def landing_of(n):
    levels = n.bit_length() - 1
    halving = min(levels, (PANEL // SUBLANES).bit_length() - 1)
    single = max(halving - 2, 0)
    rows, size = 0, PANEL
    for bits in [1] * single + [halving - single]:
        size >>= bits
        rows += ((1 << bits) - 1) * size
    return rows + (levels - halving) * SUBLANES, single + 1, levels - halving


def landed(ref, send_sem, recv_sem, peer):
    return pltpu.make_async_remote_copy(
        src_ref=ref, dst_ref=ref, send_sem=send_sem, recv_sem=recv_sem, device_id=peer, device_id_type=MESH)


def kernel(n, ncols, owner_hbm, parent, rhs_hbm, child_hbm, row_map_hbm, col_map_hbm,
           front, left, inverse, side, panel, owner, rhs_t, row_map, col_map, child,
           lead_out, lead_in, tail_out, tail_in, flat, stacked, spread_at, turned3, hot, prod, total, halves, gram, gram_in, gram_all,
           in_sem, lead_sem, tail_sem, pan_sem, gram_sem, side_sem, send_sem, recv_sem, extra_sem):
    row, col = lax.axis_index("rows"), lax.axis_index("cols")
    rows_dev, cols_dev = front.shape
    child_rows, child_cols = child.shape
    nrhs = rhs_t.shape[0]
    block = child_rows // n
    spare = cols_dev - child_cols
    other = (flipped(row, 1), col)
    first_loads = [
        pltpu.make_async_copy(source, target, in_sem.at[k])
        for k, (source, target) in enumerate([(owner_hbm, owner), (row_map_hbm, row_map), (child_hbm, child)])
    ]
    later_loads = [
        pltpu.make_async_copy(source, target, in_sem.at[3 + k])
        for k, (source, target) in enumerate([(col_map_hbm, col_map), (rhs_hbm, rhs_t), (parent, front)])
    ]
    for load in first_loads + later_loads:
        load.start()

    barrier = pltpu.get_barrier_semaphore()
    for code in reversed(range(1, n)):
        pl.semaphore_signal(barrier, inc=1, device_id=(flipped(row, code), col), device_id_type=MESH)
    for step in range(1, ncols):
        pl.semaphore_signal(barrier, inc=1, device_id=(row, lax.rem(col + step, ncols)), device_id_type=MESH)

    for load in first_loads:
        load.wait()
    source = lax.broadcasted_iota(jnp.int32, (1, child_rows), 1)
    target = jnp.zeros((1, child_rows), jnp.int32)
    for k in range(n):
        target = jnp.where(source // block == k, owner[k] * block + source % block, target)
    place = lax.broadcasted_iota(jnp.int32, (child_rows, child_rows), 0) == target
    place_f = jnp.where(place, 1.0, 0.0).astype(f32)
    landing = jnp.sum(place_f * row_map[...].astype(f32), axis=1, keepdims=True)
    place_b = place_f.astype(bf16)
    one, two, three = pieces(child[...])
    ordered = dot(place_b, one, ((1,), (0,))) + dot(place_b, two, ((1,), (0,))) + dot(place_b, three, ((1,), (0,)))
    slot_of = lax.broadcasted_iota(jnp.int32, (child_rows, LANES), 0)
    lane_of = lax.broadcasted_iota(jnp.int32, (child_rows, LANES), 1)
    spots = jnp.where(lane_of == row * block + slot_of % block, landing, 0.0)
    pick = lax.broadcasted_iota(jnp.int32, (n, child_rows), 0) == lax.broadcasted_iota(jnp.int32, (n, child_rows), 1) // block
    heads = dot_full(jnp.where(pick, 1.0, 0.0).astype(f32), spots)
    for k in range(n):
        lead_out[k, :block] = ordered[k * block : (k + 1) * block, :LANES]
        lead_out[k, block : block + 1] = heads[k : k + 1]
        tail_out[k] = ordered[k * block : (k + 1) * block, LANES:]

    pl.semaphore_wait(barrier, n - 1 + ncols - 1)

    for source_ref, target_ref, sem in ((lead_out, lead_in, lead_sem), (tail_out, tail_in, tail_sem)):
        for code in reversed(range(1, n)):
            peer = flipped(row, code)
            pltpu.make_async_remote_copy(
                src_ref=source_ref.at[peer], dst_ref=target_ref.at[row], send_sem=sem.at[0], recv_sem=sem.at[1],
                device_id=(peer, col), device_id_type=MESH).start()
    lead_in[row] = lead_out[row]
    tail_in[row] = tail_out[row]

    for load in later_loads:
        load.wait()
    cols_at = lax.broadcasted_iota(jnp.int32, hot.shape, 0)
    hot[...] = jnp.where(cols_at == col_map[...], 1.0, 0.0).astype(f32).astype(bf16)
    padded = jnp.concatenate([rhs_t[...], jnp.zeros((LANES - nrhs, rows_dev), f32)], axis=0)
    sides = jnp.transpose(padded)

    lead_all = landed(lead_in.at[pl.ds(0, n - 1)], lead_sem.at[0], lead_sem.at[1], other)
    lead_all.wait_recv()
    heads = lead_in[0, block : block + 1]
    for k in range(1, n):
        heads = heads + lead_in[k, block : block + 1]
    for k in range(n):
        flat[k * block : (k + 1) * block, :LANES] = lead_in[k, :block]
    spot = lax.broadcasted_iota(jnp.int32, (rows_dev, child_rows), 0) == heads[:, :child_rows].astype(jnp.int32)
    spot_b = jnp.where(spot, 1.0, 0.0).astype(f32).astype(bf16)
    spread_at[...] = jnp.concatenate([spot_b] * 3, axis=1)

    def assemble(vals, first, last):
        low = max(0, first - spare) // LANES * LANES
        high = min(child_cols, last)
        spread = dot(vals[:, low:high], hot[first:last, low:high], ((1,), (1,)))
        front[:, first:last] = front[:, first:last] + dot(spread_at[...], spread.astype(bf16), ((1,), (0,)))

    lead_vals = jnp.concatenate(pieces(flat[:, :LANES]), axis=0)
    assemble(lead_vals, 0, PANEL)
    pan_copies = [
        pltpu.make_async_remote_copy(
            src_ref=front.at[:, pl.ds(0, PANEL)], dst_ref=panel, send_sem=pan_sem.at[1 + step], recv_sem=pan_sem.at[0],
            device_id=(row, step), device_id_type=MESH)
        for step in range(1, ncols)
    ]

    @pl.when(col == 0)
    def _():
        for copy in pan_copies:
            copy.start()
        panel[...] = front[:, :PANEL]

    chunks = min(n, PANEL // SUBLANES)
    chunk = PANEL // chunks
    own_chunk = lax.rem(row, chunks)
    own_rows = pl.ds(pl.multiple_of(own_chunk * chunk, SUBLANES), chunk)

    def gram_step():
        turned = jnp.transpose(panel[...])
        gram[...] = dot_full(turned, panel[...])
        for code in reversed(range(1, n)):
            peer = flipped(row, code)
            start = pl.multiple_of(lax.rem(peer, chunks) * chunk, SUBLANES)
            pltpu.make_async_remote_copy(
                src_ref=gram.at[pl.ds(start, chunk)], dst_ref=gram_in.at[row],
                send_sem=gram_sem.at[0], recv_sem=gram_sem.at[1], device_id=(peer, col), device_id_type=MESH).start()
        gram_in[row] = gram[own_rows, :]
        high, low, _ = pieces(turned)
        turned3[...] = jnp.concatenate([high, high, low], axis=1)

    pl.when(col == 0)(gram_step)

    tail_all = landed(tail_in.at[pl.ds(0, n - 1)], tail_sem.at[0], tail_sem.at[1], other)
    tail_all.wait_recv()
    for k in range(n):
        flat[k * block : (k + 1) * block, LANES:] = tail_in[k]
    tail_vals = jnp.concatenate(pieces(flat[:, LANES:]), axis=0)
    stacked[...] = jnp.concatenate([lead_vals, tail_vals], axis=1)

    def assemble_block(first):
        last = min(cols_dev, first + TILE)
        assemble(stacked, max(first, PANEL), last)

    @pl.when(col != 0)
    def _():
        for first in range(0, cols_dev, TILE):
            assemble_block(first)
        pan_copies[0].wait_recv()
        gram_step()

    block_panel = panel[...]

    def product(right):
        top, rest, _ = pieces(right)
        return dot(turned3[...], jnp.concatenate([top, rest, top], axis=0), ((1,), (0,)))

    ready = [0]

    def products(last):
        while ready[0] < last:
            first = ready[0]
            upto = min(cols_dev, first + TILE)

            @pl.when(col == 0)
            def _():
                assemble_block(first)

            right = front[:, first:upto]
            if first == 0:
                right = jnp.concatenate([jnp.where(col == 0, sides, right[:, :PANEL]), right[:, PANEL:]], axis=1)
            prod[:, first:upto] = product(right)
            ready[0] = upto

    starts, parts, halving = plan(n, prod.shape[1])
    base = [row * 0] * len(parts)
    nstages = len(parts[0][0])

    def own_bit(bit):
        return (row // (1 << bit)) % 2

    def members(bits):
        mine = sum(own_bit(bit) * (1 << i) for i, bit in enumerate(bits))
        others = []
        for d in reversed(range(1, 1 << len(bits))):
            code, peer = 0, row
            for i, bit in enumerate(bits):
                own = own_bit(bit)
                flip = d >> i & 1
                code = code + (1 - own if flip else own) * (1 << i)
                peer = peer + ((1 - 2 * own) * (1 << bit) if flip else 0)
            others.append((code, peer))
        return mine, others

    def send_part(q, stage, at, size, split):
        groups, extras = parts[q]
        bits = groups[stage] if split else extras[stage]
        mine, others = members(bits)
        piece = size >> len(bits) if split else size
        keep = pl.multiple_of(base[q] + mine * piece if split else base[q], SUBLANES)
        width = starts[q + 1] - starts[q]
        send, recv = (send_sem.at[0], recv_sem.at[q, stage]) if split else (extra_sem.at[0, q, stage], extra_sem.at[1, q, stage])
        for d, (code, peer) in enumerate(others):
            give = pl.multiple_of(base[q] + code * piece, SUBLANES) if split else keep
            pltpu.make_async_remote_copy(
                src_ref=prod.at[pl.ds(give, piece), pl.ds(starts[q], width)],
                dst_ref=halves.at[q, pl.ds(at + d * piece, piece), pl.ds(0, width)],
                send_sem=send, recv_sem=recv, device_id=(peer, col), device_id_type=MESH).start()
        base[q] = keep
        return len(others), at, send, recv, keep, piece, width

    def send_stage(stage, at, size, split, before):
        held = []
        for q in range(len(parts)):
            before(q)
            if split:
                marks[q].append(base[q])
            held.append(send_part(q, stage, at, size, split))
        used, piece = held[0][0], held[0][5]
        return (held, split), at + used * piece, piece

    def adder(state):
        held, split = state

        def add_part(q):
            used, at, send, recv, keep, piece, width = held[q]
            whole = landed(halves.at[q, pl.ds(at, used * piece), pl.ds(0, width)], send, recv, other)
            whole.wait_recv()
            if not split:
                whole.wait_send()
            spot = (pl.ds(keep, piece), slice(starts[q], starts[q + 1]))
            value = prod[spot]
            for d in range(used):
                value = value + halves[q, at + d * piece : at + (d + 1) * piece, :width]
            prod[spot] = value

        return add_part

    def share_part(q, stage, piece):
        _, others = members(parts[q][0][stage])
        keep = pl.multiple_of(base[q], SUBLANES)
        columns = pl.ds(starts[q], starts[q + 1] - starts[q])
        spot = total.at[pl.ds(keep, piece), columns]
        recv = recv_sem.at[q, nstages + stage]
        for _, peer in others:
            pltpu.make_async_remote_copy(
                src_ref=spot, dst_ref=spot, send_sem=send_sem.at[1], recv_sem=recv,
                device_id=(peer, col), device_id_type=MESH).start()
        return landed(total.at[pl.ds(0, len(others) * piece), columns], send_sem.at[1], recv, other)

    marks = [[] for _ in parts]
    at, size = 0, PANEL
    held, at, size = send_stage(0, at, size, True, lambda q: products(starts[q + 1]))

    gathered = landed(gram_in.at[pl.ds(0, n - 1)], gram_sem.at[0], gram_sem.at[1], other)
    gathered.wait_recv()
    summed = gram_in[0]
    for k in range(1, n):
        summed = summed + gram_in[k]
    gram_all[own_rows, :] = summed
    for code in reversed(range(1, chunks)):
        peer = row - own_chunk + flipped(own_chunk, code)
        pltpu.make_async_remote_copy(
            src_ref=gram_all.at[own_rows], dst_ref=gram_all.at[own_rows],
            send_sem=gram_sem.at[2], recv_sem=gram_sem.at[3], device_id=(peer, col), device_id_type=MESH).start()

    for stage in range(1, nstages):
        held, at, size = send_stage(stage, at, size, True, adder(held))
    spread_all = landed(gram_all.at[pl.ds(0, (chunks - 1) * chunk)], gram_sem.at[2], gram_sem.at[3], other)
    spread_all.wait_recv()
    turns = PANEL // SUBLANES
    mat, done = gram_all[...], 0

    def turn_by(mat, done, share):
        upto = min(turns, done + share)
        return (sweep_groups(mat, upto - done) if upto > done else mat), upto

    mat, done = turn_by(mat, done, SHARES[0])
    for stage in range(len(parts[0][1])):
        held, at, size = send_stage(stage, at, size, False, adder(held))
    last_add = adder(held)
    waiting = [None for _ in parts]
    for stage in reversed(range(nstages)):
        for q in range(len(parts)):
            if stage == nstages - 1:
                last_add(q)
                spot = (pl.ds(pl.multiple_of(base[q], SUBLANES), size), slice(starts[q], starts[q + 1]))
                total[spot] = prod[spot]
            else:
                waiting[q].wait_recv()
            waiting[q] = share_part(q, stage, size)
            base[q] = marks[q][stage]
        mat, done = turn_by(mat, done, turns if stage == 0 else SHARES[1 + nstages - 1 - stage])
        size <<= len(parts[0][0][stage])

    inverse[...] = -mat
    high, low, _ = pieces(dot_full(block_panel, -mat))
    left3 = jnp.concatenate([high, high, low], axis=1)
    left[...] = left3
    @pl.when(col == 0)
    def _():
        for copy in pan_copies:
            copy.wait_send()

    updated_to = 0
    for q in range(len(parts)):
        waiting[q].wait_recv()
        if q == 0:
            side_copies = [
                pltpu.make_async_remote_copy(
                    src_ref=side, dst_ref=side, send_sem=side_sem.at[1 + step], recv_sem=side_sem.at[0],
                    device_id=(row, step), device_id_type=MESH)
                for step in range(1, ncols)
            ]

            @pl.when(col == 0)
            def _():
                side[...] = total[:, :PANEL]
                for copy in side_copies:
                    copy.start()

        upto = starts[q + 1] // TILE * TILE if q < len(parts) - 1 else starts[q + 1]
        for first in range(updated_to, upto, TILE):
            last = min(first + TILE, upto)
            right = total[:, first:last]
            if first == 0:
                right = jnp.concatenate([jnp.where(col == 0, gram_all[...], right[:, :PANEL]), right[:, PANEL:]], axis=1)
            top, rest, _ = pieces(right)
            front[:, first:last] = front[:, first:last] - dot(left3, jnp.concatenate([top, rest, top], axis=0), ((1,), (0,)))
        updated_to = upto

    lead_all.wait_send()
    tail_all.wait_send()
    gathered.wait_send()
    spread_all.wait_send()
    for k in range(2):
        landed(total.at[pl.ds(0, PANEL - (PANEL >> halving))], send_sem.at[k], send_sem.at[k], other).wait_send()

    @pl.when(col == 0)
    def _():
        for copy in side_copies:
            copy.wait_send()

    @pl.when(col != 0)
    def _():
        side_copies[0].wait_recv()


def finish(front, left, inverse, side, rhs_t, updated, side_out, left_out, side_t, left_t, sems):
    nrhs, rows_dev = rhs_t.shape
    count = sems.shape[0] - 2
    part = rows_dev // count
    copies = [
        pltpu.make_async_copy(front.at[pl.ds(k * part, part)], updated.at[pl.ds(k * part, part)], sems.at[k])
        for k in range(count)
    ]
    for copy in copies:
        copy.start()
    sides = side[...]
    side_t[...] = jnp.transpose(dot_full(inverse[...], sides))[:nrhs]
    top, rest, _ = pieces(sides)
    fitted = dot(left[...], jnp.concatenate([top, rest, top], axis=0), ((1,), (0,)))
    left_t[...] = rhs_t[...] - jnp.transpose(fitted)[:nrhs]
    for k, (source, target) in enumerate([(side_t, side_out), (left_t, left_out)]):
        copies.append(pltpu.make_async_copy(source, target, sems.at[count + k]))
        copies[-1].start()
    for copy in copies:
        copy.wait()


def solution(mesh):
    n, ncols = mesh.shape["rows"], mesh.shape["cols"]

    def shards(parent_front, right_sides, child_values, block_owner, row_map, col_map):
        rows_dev, cols_dev = parent_front.shape
        child_rows, child_cols = child_values.shape
        nrhs = right_sides.shape[1]
        starts, parts, _ = plan(n, cols_dev)
        nparts = len(parts)
        widest = max(starts[q + 1] - starts[q] for q in range(nparts))
        landing_rows, nstages, nextra = landing_of(n)
        block = child_rows // n
        chunks = min(n, PANEL // SUBLANES)
        vmem = pl.BlockSpec(memory_space=pltpu.VMEM)
        dma = pltpu.SemaphoreType.DMA
        hbm = pl.BlockSpec(memory_space=pltpu.HBM)
        rhs_t = right_sides.T
        operands = (block_owner, parent_front, rhs_t, child_values, row_map.reshape(1, -1), col_map.reshape(1, -1))
        front, left, inverse, side = pl.pallas_call(
            functools.partial(kernel, n, ncols),
            out_shape=(
                pltpu.VMEM((rows_dev, cols_dev), f32),
                pltpu.VMEM((rows_dev, 3 * PANEL), bf16),
                pltpu.VMEM((PANEL, PANEL), f32),
                pltpu.VMEM((PANEL, LANES), f32),
            ),
            in_specs=[hbm] * 6,
            out_specs=(vmem,) * 4,
            scratch_shapes=[
                pltpu.VMEM((rows_dev, PANEL), f32),
                pltpu.SMEM(block_owner.shape, jnp.int32),
                pltpu.VMEM((nrhs, rows_dev), f32),
                pltpu.VMEM((1, child_rows), jnp.int32),
                pltpu.VMEM((1, child_cols), jnp.int32),
                pltpu.VMEM((child_rows, child_cols), f32),
                pltpu.VMEM((n, block + 1, LANES), f32),
                pltpu.VMEM((n, block + 1, LANES), f32),
                pltpu.VMEM((n, block, child_cols - LANES), f32),
                pltpu.VMEM((n, block, child_cols - LANES), f32),
                pltpu.VMEM((child_rows, child_cols), f32),
                pltpu.VMEM((3 * child_rows, child_cols), bf16),
                pltpu.VMEM((rows_dev, 3 * child_rows), bf16),
                pltpu.VMEM((PANEL, 3 * rows_dev), bf16),
                pltpu.VMEM((cols_dev, child_cols), bf16),
                pltpu.VMEM((PANEL, cols_dev), f32),
                pltpu.VMEM((PANEL, cols_dev), f32),
                pltpu.VMEM((nparts, landing_rows, widest), f32),
                pltpu.VMEM((PANEL, PANEL), f32),
                pltpu.VMEM((n, PANEL // chunks, PANEL), f32),
                pltpu.VMEM((PANEL, PANEL), f32),
                dma((6,)),
                dma((2,)),
                dma((2,)),
                dma((ncols + 1,)),
                dma((4,)),
                dma((ncols + 1,)),
                dma((2,)),
                dma((nparts, 2 * nstages)),
                dma((2, nparts, nextra) if nextra else (1,)),
            ],
            compiler_params=pltpu.CompilerParams(collective_id=0, has_side_effects=True, vmem_limit_bytes=VMEM_LIMIT),
        )(*[pltpu.with_memory_space_constraint(value, pltpu.HBM) for value in operands])
        updated, side_t, left_t = pl.pallas_call(
            finish,
            out_shape=(
                jax.ShapeDtypeStruct((rows_dev, cols_dev), f32),
                jax.ShapeDtypeStruct((nrhs, PANEL), f32),
                jax.ShapeDtypeStruct((nrhs, rows_dev), f32),
            ),
            in_specs=[vmem] * 5,
            out_specs=(hbm, hbm, hbm),
            scratch_shapes=[
                pltpu.VMEM((nrhs, PANEL), f32),
                pltpu.VMEM((nrhs, rows_dev), f32),
                dma((6,)),
            ],
            compiler_params=pltpu.CompilerParams(vmem_limit_bytes=VMEM_LIMIT),
        )(front, left, inverse, side, rhs_t)
        return updated, side_t.T, left_t.T

    in_specs = (
        P("rows", "cols"),
        P("rows", None),
        P("rows", "cols"),
        P("rows"),
        P("rows"),
        P("cols"),
    )
    out_specs = (P("rows", "cols"), P(), P("rows", None))
    return jax.shard_map(shards, mesh=mesh, in_specs=in_specs, out_specs=out_specs, check_vma=False)
```
